512 devices in a mesh: lat: 8 (over z), lon: 64 (over y, x, core).
Axes of the slice: x: 4, y: 8, z: 8, core: 2. Of those that a mesh axis runs over, the one named last changes fastest.
Arguments:
- field: bfloat16 [512, 2048, 128], P('lat', 'lon'), may hold values from -6 to 6
- land_mask: int32 [512, 2048], P('lat', 'lon'), may hold values 0 or 1
- zonal_tap_weight: float32 [15, 128], replicated, may hold values from -1.5 to 1.5
- norm_gain: float32 [128], replicated, may hold values from 0.1 to 1.9
- up_weight: bfloat16 [128, 512], replicated, may hold values from -0.5 to 0.5
- down_weight: bfloat16 [512, 128], replicated, may hold values from -0.25 to 0.25
- polar_rows: int32 [256], P('lat'), may hold values from 0 to 63, as said below
- polar_owner: int32 [256], P('lat'), may hold values from 0 to 63, as said below
- polar_taps: float32 [31], replicated, may hold values from -0.8 to 0.8
Outputs:
- mixed_field: bfloat16 [512, 2048, 128], P('lat', 'lon')
- polar_field: bfloat16 [1024, 2048, 128], P(('lat', 'lon'))
The draws below stay inside these ranges and needn't reach their ends.
Inputs may be any that keep to these rules, and one draw needn't show every extreme that they name: `polar_rows`: within each band the 32 entries are distinct rows in increasing order. `polar_owner`: within each band no owner is named by more than 2 entries, and some owner by exactly 2.
All inputs are finite; a program needn't handle non-finite values. No bound on the sum of `land_mask` on one device may be relied on, other than what follows from the above.
Results may differ from the reference program's by a relative error of at most 0.0059.
Values may be sent and summed in bfloat16 or wider, within the bound.
A program may use at most 64 MiB of HBM per device.

```python
import jax
import jax.numpy as jnp
from jax import lax

C = 128
HID = 512
ZTAPS = 15
DILATION_STEP = 4
FTAPS = 31
LAT_DEV = 64
TILES_LON = 64
NLAT = 512
NLON = 2048
PROWS = 32
PROWS_ALL = 256
PMAX = 2
N_LAT = 8
N_LON = 64


def draw_polar_rows(key, part):
    band_count = PROWS_ALL // PROWS

    def one_band(band):
        band_key = jax.random.fold_in(key, band)
        scores = jax.random.permutation(band_key, LAT_DEV)
        row_ids = jnp.arange(LAT_DEV)
        forced = (row_ids == 0) | (row_ids == LAT_DEV - 1)
        scores = jnp.where(forced, -1 - row_ids, scores)
        chosen = jnp.argsort(scores, stable=True)[:PROWS]
        return jnp.sort(chosen)
    picked = jax.vmap(one_band)(jnp.arange(band_count))
    return picked.reshape(-1).astype(jnp.int32)


def draw_polar_owner(key, part):
    band_count = PROWS_ALL // PROWS
    slot_count = TILES_LON * PMAX

    def one_band(band):
        band_key = jax.random.fold_in(jax.random.fold_in(key, 7919), band)
        first_key, second_key, third_key = jax.random.split(band_key, 3)
        drawn_owner = jax.random.randint(first_key, (), 0, TILES_LON)
        full_owner = jnp.where(band == 0, TILES_LON - 1, drawn_owner)
        slot_ids = jnp.arange(slot_count)
        scores = jax.random.permutation(second_key, slot_count)
        scores = jnp.where(slot_ids // PMAX == full_owner, -1 - slot_ids, scores)
        chosen = jnp.argsort(scores, stable=True)[:PROWS]
        owners = chosen // PMAX
        return jax.random.permutation(third_key, owners)
    picked = jax.vmap(one_band)(jnp.arange(band_count))
    return picked.reshape(-1).astype(jnp.int32)


def touch_ends(drawn, stream_key, low, high):
    longest = drawn.shape.index(max(drawn.shape))
    spots = []
    for shift in (0, 1):
        where = [jax.random.randint(jax.random.fold_in(stream_key, axis), (), 0, length) for axis, length in enumerate(drawn.shape)]
        where[longest] = (where[longest] + shift) % drawn.shape[longest]
        spots.append(tuple(where))
    return drawn.at[spots[0]].set(low).at[spots[1]].set(high)


def levels(key, extent, cuts, least, top_value):
    factor_of, own = 1.0, jax.random.fold_in(key, 6)
    for position, parts in cuts:
        draws = jnp.exp(jax.random.uniform(jax.random.fold_in(own, position), (parts,), jnp.float32, least / len(cuts), top_value / len(cuts)))
        factor_of = factor_of * jnp.repeat(draws, extent[position] // parts).reshape([-1 if axis == position else 1 for axis in range(len(extent))])
    return factor_of


def bell_draw(rng, extent, deviation, most, cuts=(), kind=jnp.bfloat16):
    result = deviation * jax.random.normal(rng, extent, jnp.float32)
    if cuts:
        result = result * levels(rng, extent, cuts, -0.22, 0.18)
    return jnp.clip(result, -most, most).astype(kind)


def setup_inputs(seed: int = 0) -> dict:
    key_list = jax.random.split(jax.random.key(seed), 10)
    field = bell_draw(key_list[0], (NLAT, NLON, C), 1.0, 6.0, ((0, 8), (1, 64)))
    land_mask = touch_ends((jax.random.randint(key_list[1], (NLAT, NLON), 0, 4) < 3).astype(jnp.int32), jax.random.fold_in(key_list[1], 1), 0, 1)
    zonal_tap_weight = bell_draw(key_list[2], (ZTAPS, C), ZTAPS ** -0.5, 1.5, (), jnp.float32)
    norm_gain = jnp.clip(1.0 + 0.18 * jax.random.normal(key_list[3], (C,), jnp.float32), 0.1, 1.9)
    up_weight = bell_draw(key_list[4], (C, HID), C ** -0.5, 0.5)
    down_weight = bell_draw(key_list[5], (HID, C), HID ** -0.5, 0.25)
    polar_rows = draw_polar_rows(jax.random.fold_in(key_list[9], 71), 0)
    polar_owner = draw_polar_owner(jax.random.fold_in(key_list[9], 71), 0)
    polar_taps = bell_draw(key_list[8], (FTAPS,), 0.2, 0.8, (), jnp.float32)
    return {"field": field, "land_mask": land_mask, "zonal_tap_weight": zonal_tap_weight, "norm_gain": norm_gain, "up_weight": up_weight, "down_weight": down_weight, "polar_rows": polar_rows, "polar_owner": polar_owner, "polar_taps": polar_taps}


def zonal_mix(block, zonal_tap_weight, norm_gain, up_weight, down_weight):
    source_column = block.astype(jnp.float32)
    tap_sum_output = jnp.zeros(source_column.shape, jnp.float32)
    half_tap_count = zonal_tap_weight.shape[0] // 2
    for zonal_tap_index in range(zonal_tap_weight.shape[0]):
        tap_sum_output = tap_sum_output + zonal_tap_weight[zonal_tap_index] * jnp.roll(source_column, -(zonal_tap_index - half_tap_count) * DILATION_STEP, axis=1)
    average = lax.optimization_barrier(jnp.mean(tap_sum_output, axis=-1, keepdims=True))
    centred = tap_sum_output - average
    variance = lax.optimization_barrier(jnp.mean(centred * centred, axis=-1, keepdims=True))
    normed = (centred * lax.rsqrt(variance + 1e-06) * norm_gain).astype(jnp.bfloat16)
    flat_cells = normed.reshape(-1, normed.shape[-1])
    hidden = jax.nn.gelu(jnp.dot(flat_cells, up_weight, preferred_element_type=jnp.float32)).astype(jnp.bfloat16)
    branch = jnp.dot(hidden, down_weight, preferred_element_type=jnp.float32).astype(jnp.bfloat16)
    return branch.reshape(block.shape)

def reference(field, land_mask, zonal_tap_weight, norm_gain, up_weight, down_weight, polar_rows, polar_owner, polar_taps):
    mask_half = land_mask.astype(jnp.bfloat16)[:, :, None]
    masked = field * mask_half
    block_rows = LAT_DEV // N_LON
    blocks = masked.reshape(NLAT // block_rows, block_rows, NLON, C)
    branch = lax.map(lambda block: zonal_mix(block, zonal_tap_weight, norm_gain, up_weight, down_weight), blocks)
    branch = branch.reshape(NLAT, NLON, C)
    mixed_field = ((masked.astype(jnp.float32) + branch.astype(jnp.float32)) * mask_half.astype(jnp.float32)).astype(jnp.bfloat16)
    entries = jnp.arange(PROWS_ALL).astype(jnp.int32)
    band_index = (entries // PROWS).astype(jnp.int32)
    same_owner = (polar_owner[:, None] == polar_owner[None, :]) & (band_index[:, None] == band_index[None, :]) & (entries[None, :] < entries[:, None])
    slot_rank = lax.optimization_barrier(jnp.sum(same_owner.astype(jnp.int32), axis=1)).astype(jnp.int32)
    destination = ((band_index * N_LON + polar_owner) * PMAX + slot_rank).astype(jnp.int32)
    global_rows = (band_index * LAT_DEV + polar_rows).astype(jnp.int32)
    half_filter = polar_taps.shape[0] // 2

    def filter_row(row_index):
        circle = lax.dynamic_index_in_dim(mixed_field, row_index, 0, keepdims=False).astype(jnp.float32)
        tap_sum_output = jnp.zeros(circle.shape, jnp.float32)
        for zonal_tap_index in range(polar_taps.shape[0]):
            tap_sum_output = tap_sum_output + polar_taps[zonal_tap_index] * jnp.roll(circle, -(zonal_tap_index - half_filter), axis=0)
        return tap_sum_output.astype(jnp.bfloat16)
    filtered = lax.map(filter_row, global_rows)
    polar_field = jnp.zeros((N_LAT * N_LON * PMAX, NLON, C), jnp.bfloat16).at[destination].set(filtered)
    return (mixed_field, polar_field)
```

```python
import functools

import jax
import jax.numpy as jnp
from jax import lax
from jax.experimental import pallas as pl
from jax.experimental.pallas import tpu as pltpu
from jax.sharding import PartitionSpec as P

DILATION = 4
LAND = 64.0
GELU_A = 0.7978845608028654
GELU_B = 0.044715 * GELU_A


def vmem():
    return pl.BlockSpec(memory_space=pltpu.VMEM)


def smem():
    return pl.BlockSpec(memory_space=pltpu.SMEM)


def mix(tiles, keep, taps, gain, up, down):
    rows = tiles.shape[0]
    channels = tiles.shape[-1]
    land = tiles == LAND
    tiles = jnp.where(land, 0.0, tiles)
    turned = pltpu.roll(tiles.reshape(rows * (keep + 8), 8, channels), 4, 1).reshape(tiles.shape)
    first_half = lax.broadcasted_iota(jnp.int32, (rows, keep + 7, 8, channels), 2) < 4
    halves = jnp.where(first_half, turned[:, :-1], turned[:, 1:])
    zonal = None
    for k in range(taps.shape[0]):
        start = (k - 7) * DILATION + 32
        source = halves if start % 8 else tiles
        term = taps[k][None, None, None, :] * source[:, start // 8 : start // 8 + keep]
        zonal = term if zonal is None else zonal + term
    zonal = zonal.reshape(rows * keep * 8, channels)
    centred = zonal - jnp.mean(zonal, axis=-1, keepdims=True)
    variance = jnp.mean(centred * centred, axis=-1, keepdims=True)
    normed = (centred * lax.rsqrt(variance + 1e-06) * gain).astype(jnp.bfloat16)
    hidden = jnp.dot(normed, up, preferred_element_type=jnp.float32)
    bent = jnp.tanh(hidden * (GELU_A + GELU_B * (hidden * hidden)))
    half = 0.5 * hidden
    hidden = (half + half * bent).astype(jnp.bfloat16)
    branch = jnp.dot(hidden, down, preferred_element_type=jnp.float32).astype(jnp.bfloat16)
    centre = slice(4, 4 + keep)
    mixed = tiles[:, centre].reshape(-1, channels) + branch.astype(jnp.float32)
    return jnp.where(land[:, centre].reshape(-1, channels), 0.0, mixed).astype(jnp.bfloat16)


def prepare_kernel(rows_ref, owner_ref, field_ref, mask_ref, coded_ref, send_ref, table):
    lat_rows, cols, channels = field_ref.shape
    owners = send_ref.shape[0]
    for r in range(0, lat_rows, 8):
        wet = mask_ref[r : r + 8][:, :, None]
        coded_ref[r : r + 8] = jnp.where(
            jnp.broadcast_to(wet, (8, cols, channels)) != 0,
            field_ref[r : r + 8].astype(jnp.float32),
            LAND,
        ).astype(jnp.bfloat16)
    send_ref[...] = jnp.full_like(send_ref, LAND)

    @pl.loop(0, owners)
    def _(o):
        table[o] = 0

    @pl.loop(0, rows_ref.shape[0])
    def _(e):
        owner = owner_ref[e]
        rank = table[owner]
        table[owner] = rank + 1
        send_ref[owner, rank] = coded_ref[rows_ref[e]]


def prepare(field, land_mask, polar_rows, polar_owner, owners, slots):
    lat_rows, cols, channels = field.shape
    return pl.pallas_call(
        prepare_kernel,
        out_shape=(
            jax.ShapeDtypeStruct(field.shape, jnp.bfloat16),
            jax.ShapeDtypeStruct((owners, slots, cols, channels), jnp.bfloat16),
        ),
        in_specs=[smem(), smem(), vmem(), vmem()],
        out_specs=(vmem(), vmem()),
        scratch_shapes=[pltpu.SMEM((owners,), jnp.int32)],
    )(polar_rows, polar_owner, field, land_mask)


def own_kernel(left_ref, own_ref, right_ref, taps_ref, gain_ref, up_ref, down_ref, out_ref):
    lat_rows, cols, channels = own_ref.shape
    step = 8

    @pl.loop(0, lat_rows // step)
    def _(i):
        rows = pl.ds(i * step, step)
        tiles = jnp.concatenate(
            [
                ref[rows].astype(jnp.float32).reshape(step, cols // 8, 8, channels)
                for ref in (left_ref, own_ref, right_ref)
            ],
            axis=1,
        )
        mixed = mix(tiles, cols // 8, taps_ref, gain_ref[...], up_ref[...], down_ref[...])
        out_ref[rows] = mixed.reshape(step, cols, channels)


def own(left, coded, right, taps, gain, up, down):
    return pl.pallas_call(
        own_kernel,
        out_shape=jax.ShapeDtypeStruct(coded.shape, jnp.bfloat16),
        in_specs=[vmem()] * 7,
        out_specs=vmem(),
    )(left, coded, right, taps, gain, up, down)


def polar_kernel(raw_ref, taps_ref, gain_ref, up_ref, down_ref, line_ref, out_ref, padded, mixed):
    tiles, slots, cols, channels = raw_ref.shape
    length = tiles * cols
    chunk = 256
    block = 128
    wide = block + 2 * cols
    band = pltpu.roll(jnp.broadcast_to(line_ref[...], (block, 256)), 0, 1, stride=1, stride_axis=0)
    band = band[:, :wide]
    high = band.astype(jnp.bfloat16)
    low = (band - high.astype(jnp.float32)).astype(jnp.bfloat16)
    for s in range(slots):
        padded[0:cols] = raw_ref[tiles - 1, s]
        padded[cols + length : length + 2 * cols] = raw_ref[0, s]
        padded[cols : cols + length] = raw_ref[:, s].reshape(length, channels)

        @pl.loop(0, length // chunk)
        def _(i):
            at = pl.multiple_of(i * chunk, chunk)
            tile = padded[pl.ds(at, chunk + 2 * cols)].astype(jnp.float32)
            tile = tile.reshape(1, (chunk + 2 * cols) // 8, 8, channels)
            mixed[pl.ds(cols + at, chunk)] = mix(
                tile, chunk // 8, taps_ref, gain_ref[...], up_ref[...], down_ref[...]
            )

        mixed[0:cols] = mixed[length : length + cols]
        mixed[cols + length : length + 2 * cols] = mixed[cols : 2 * cols]

        @pl.loop(0, length // block)
        def _(i):
            at = pl.multiple_of(i * block, block)
            window = mixed[pl.ds(at, wide)]
            total = jnp.dot(high, window, preferred_element_type=jnp.float32)
            total += jnp.dot(low, window, preferred_element_type=jnp.float32)
            out_ref[s, pl.ds(at, block)] = total.astype(jnp.bfloat16)


def polar(raw, taps, gain, up, down, line):
    tiles, slots, cols, channels = raw.shape
    length = tiles * cols
    return pl.pallas_call(
        polar_kernel,
        out_shape=jax.ShapeDtypeStruct((slots, length, channels), jnp.bfloat16),
        in_specs=[vmem()] * 6,
        out_specs=vmem(),
        scratch_shapes=[
            pltpu.VMEM((length + 2 * cols, channels), jnp.bfloat16),
            pltpu.VMEM((length + 2 * cols, channels), jnp.bfloat16),
        ],
    )(raw, taps, gain, up, down, line)


def body(field, land_mask, taps, gain, up, down, polar_rows, polar_owner, polar_taps):
    owners = lax.axis_size("lon")
    slots = 2
    gain = gain[None, :]
    coded, outgoing = prepare(field, land_mask, polar_rows, polar_owner, owners, slots)
    raw = lax.all_to_all(outgoing, "lon", split_axis=0, concat_axis=0, tiled=True)
    ahead = [(i, (i + 1) % owners) for i in range(owners)]
    back = [(i, (i - 1) % owners) for i in range(owners)]
    left = lax.ppermute(coded, "lon", ahead)
    right = lax.ppermute(coded, "lon", back)
    mixed_field = own(left, coded, right, taps, gain, up, down)
    cols = field.shape[1]
    half = polar_taps.shape[0] // 2
    line = jnp.zeros((1, 256), jnp.float32)
    line = lax.dynamic_update_slice(line, polar_taps[None, :], (0, cols - half))
    polar_field = polar(raw, taps, gain, up, down, line)
    return (mixed_field, polar_field)


def solution(mesh):
    in_specs = (P("lat", "lon", None), P("lat", "lon"), P(), P(), P(), P(), P("lat"), P("lat"), P())
    out_specs = (P("lat", "lon", None), P(("lat", "lon"), None, None))
    return jax.shard_map(body, mesh=mesh, in_specs=in_specs, out_specs=out_specs, check_vma=False)
```

```python
import functools

import jax
import jax.numpy as jnp
from jax import lax
from jax.experimental import pallas as pl
from jax.experimental.pallas import tpu as pltpu
from jax.sharding import PartitionSpec as P

DILATION = 4
LAND = 64.0
MESH = pl.DeviceIdType.MESH
GELU_A = 0.7978845608028654
GELU_B = 0.044715 * GELU_A


def vmem():
    return pl.BlockSpec(memory_space=pltpu.VMEM)


def smem():
    return pl.BlockSpec(memory_space=pltpu.SMEM)


def mix(tiles, keep, taps, gain, up, down):
    rows = tiles.shape[0]
    channels = tiles.shape[-1]
    land = tiles == LAND
    tiles = jnp.where(land, 0.0, tiles)
    turned = pltpu.roll(tiles.reshape(rows * (keep + 8), 8, channels), 4, 1).reshape(tiles.shape)
    first_half = lax.broadcasted_iota(jnp.int32, (rows, keep + 7, 8, channels), 2) < 4
    halves = jnp.where(first_half, turned[:, :-1], turned[:, 1:])
    zonal = None
    for k in range(taps.shape[0]):
        start = (k - 7) * DILATION + 32
        source = halves if start % 8 else tiles
        term = taps[k][None, None, None, :] * source[:, start // 8 : start // 8 + keep]
        zonal = term if zonal is None else zonal + term
    zonal = zonal.reshape(rows * keep * 8, channels)
    centred = zonal - jnp.mean(zonal, axis=-1, keepdims=True)
    variance = jnp.mean(centred * centred, axis=-1, keepdims=True)
    normed = (centred * lax.rsqrt(variance + 1e-06) * gain).astype(jnp.bfloat16)
    hidden = jnp.dot(normed, up, preferred_element_type=jnp.float32)
    bent = jnp.tanh(hidden * (GELU_A + GELU_B * (hidden * hidden)))
    half = 0.5 * hidden
    hidden = (half + half * bent).astype(jnp.bfloat16)
    branch = jnp.dot(hidden, down, preferred_element_type=jnp.float32).astype(jnp.bfloat16)
    centre = slice(4, 4 + keep)
    mixed = tiles[:, centre].reshape(-1, channels) + branch.astype(jnp.float32)
    return jnp.where(land[:, centre].reshape(-1, channels), 0.0, mixed).astype(jnp.bfloat16)


def prepare_kernel(rows_ref, owner_ref, field_ref, mask_ref, coded_ref, send_ref, table):
    lat_rows, cols, channels = field_ref.shape
    owners = send_ref.shape[0]
    for r in range(0, lat_rows, 8):
        wet = mask_ref[r : r + 8][:, :, None]
        coded_ref[r : r + 8] = jnp.where(
            jnp.broadcast_to(wet, (8, cols, channels)) != 0,
            field_ref[r : r + 8].astype(jnp.float32),
            LAND,
        ).astype(jnp.bfloat16)
    send_ref[...] = jnp.full_like(send_ref, LAND)

    @pl.loop(0, owners)
    def _(o):
        table[o] = 0

    @pl.loop(0, rows_ref.shape[0])
    def _(e):
        owner = owner_ref[e]
        rank = table[owner]
        table[owner] = rank + 1
        send_ref[owner, rank] = coded_ref[rows_ref[e]]


def prepare(field, land_mask, polar_rows, polar_owner, owners, slots):
    lat_rows, cols, channels = field.shape
    return pl.pallas_call(
        prepare_kernel,
        out_shape=(
            jax.ShapeDtypeStruct(field.shape, jnp.bfloat16),
            jax.ShapeDtypeStruct((owners, slots, cols, channels), jnp.bfloat16),
        ),
        in_specs=[smem(), smem(), vmem(), vmem()],
        out_specs=(vmem(), vmem()),
        scratch_shapes=[pltpu.SMEM((owners,), jnp.int32)],
    )(polar_rows, polar_owner, field, land_mask)


def exchange_kernel(
    near_first,
    coded_ref,
    send_ref,
    taps_ref,
    gain_ref,
    up_ref,
    down_ref,
    out_ref,
    mixed_ref,
    left,
    right,
    pieces,
    send_sem,
    piece_sem,
    halo_sem,
):
    lat_rows, cols, channels = coded_ref.shape
    owners, slots = send_ref.shape[:2]
    group = 8
    groups = owners // group
    band = lax.axis_index("lat")
    me = lax.axis_index("lon")
    mine, low = lax.div(me, group), lax.rem(me, group)
    ahead, behind = lax.rem(me + 1, owners), lax.rem(me + owners - 1, owners)
    shift = groups // 2 if near_first else 0

    def span(tile, tiles):
        return pl.ds(pl.multiple_of(tile * cols, cols), tiles * cols)

    def piece_copy(position, other):
        relative = lax.rem(position - shift + groups, groups)
        target = lax.rem(mine - relative + groups, groups) * group + lax.rem(low + other, group)
        return pltpu.make_async_remote_copy(
            src_ref=send_ref.at[target],
            dst_ref=pieces.at[:, span(position * group + low, 1)],
            send_sem=send_sem.at[0],
            recv_sem=piece_sem.at[position],
            device_id=(band, target),
            device_id_type=MESH,
        )

    def halo_copy(side, target, k):
        return pltpu.make_async_remote_copy(
            src_ref=coded_ref,
            dst_ref=side,
            send_sem=send_sem.at[1 + k],
            recv_sem=halo_sem.at[k],
            device_id=(band, target),
            device_id_type=MESH,
        )

    barrier = pltpu.get_barrier_semaphore()

    @pl.loop(1, owners)
    def _(i):
        pl.semaphore_signal(
            barrier,
            inc=1,
            device_id=(band, lax.rem(me + i, owners)),
            device_id_type=MESH,
        )

    own_position = shift if near_first else groups
    pieces[:, span(own_position * group + low, 1)] = send_ref[me]
    pl.semaphore_wait(barrier, owners - 1)

    to_ahead = halo_copy(left, ahead, 0)
    to_behind = halo_copy(right, behind, 1)
    to_ahead.start()
    to_behind.start()
    middle = groups // 2
    order = [middle]
    for q in range(1, middle):
        order += [middle - q, middle + q]
    order += [groups]
    for position in order:

        @pl.loop(1 if position == own_position else 0, group)
        def _(other, position=position):
            piece_copy(position, other).start()

    to_ahead.wait_recv()
    to_behind.wait_recv()
    step = 8

    @pl.loop(0, lat_rows // step)
    def _(i):
        rows = pl.ds(i * step, step)
        tiles = jnp.concatenate(
            [
                ref[rows].astype(jnp.float32).reshape(step, cols // 8, 8, channels)
                for ref in (left, coded_ref, right)
            ],
            axis=1,
        )
        mixed = mix(tiles, cols // 8, taps_ref, gain_ref[...], up_ref[...], down_ref[...])
        out_ref[rows] = mixed.reshape(step, cols, channels)

    def arrived(position, tiles):
        landed = pieces.at[:, span(position * group, tiles)]
        pltpu.make_async_copy(landed, landed, piece_sem.at[position]).wait()

    chunk = 4

    def mix_chunk(tile):
        keep = chunk * cols // 8
        tiles = pieces[:, span(tile - 1, chunk + 2)].astype(jnp.float32)
        tiles = tiles.reshape(slots, keep + 8, 8, channels)
        mixed = mix(tiles, keep, taps_ref, gain_ref[...], up_ref[...], down_ref[...])
        mixed_ref[:, span(tile, chunk)] = mixed.reshape(slots, chunk * cols, channels)

    arrived(middle, group - 1 if own_position == middle else group)
    mix_chunk(middle * group + 2)

    @pl.loop(1, middle)
    def _(q):
        arrived(middle - q, group)
        arrived(middle + q, group)

        @pl.loop(0, 4)
        def _(k):
            side = lax.div(k, 2)
            first = side * (middle * group + 6 + (q - 1) * group)
            first += (1 - side) * (middle * group + 2 - q * group)
            mix_chunk(first + lax.rem(k, 2) * chunk)

    arrived(groups, group - 1 if own_position == groups else group)
    ring = owners
    pieces[:, span(group + ring, 3)] = pieces[:, span(group, 3)]

    @pl.loop(0, 3)
    def _(k):
        mix_chunk(group + ring - 10 + k * chunk)

    mixed_ref[:, span(ring + 10, 3)] = mixed_ref[:, span(10, 3)]

    to_ahead.wait_send()
    to_behind.wait_send()
    sent = send_ref.at[pl.ds(0, owners - 1)]
    pltpu.make_async_copy(sent, sent, send_sem.at[0]).wait()


NEAR_FIRST = False


def exchange(coded, outgoing, taps, gain, up, down):
    owners, slots, cols, channels = outgoing.shape
    return pl.pallas_call(
        functools.partial(exchange_kernel, NEAR_FIRST),
        out_shape=(
            jax.ShapeDtypeStruct(coded.shape, jnp.bfloat16),
            jax.ShapeDtypeStruct((slots, (owners + 13) * cols, channels), jnp.bfloat16),
        ),
        in_specs=[vmem()] * 6,
        out_specs=(vmem(), vmem()),
        scratch_shapes=[
            pltpu.VMEM(coded.shape, jnp.bfloat16),
            pltpu.VMEM(coded.shape, jnp.bfloat16),
            pltpu.VMEM((slots, (owners + 11) * cols, channels), jnp.bfloat16),
            pltpu.SemaphoreType.DMA((3,)),
            pltpu.SemaphoreType.DMA((9,)),
            pltpu.SemaphoreType.DMA((2,)),
        ],
        compiler_params=pltpu.CompilerParams(collective_id=0, has_side_effects=True),
    )(coded, outgoing, taps, gain, up, down)


def filter_kernel(first_ref, mixed_ref, line_ref, out_ref):
    slots, length, channels = out_ref.shape
    cols = 32
    block = 128
    wide = block + 2 * cols
    band = pltpu.roll(jnp.broadcast_to(line_ref[...], (block, 256)), 0, 1, stride=1, stride_axis=0)
    band = band[:, :wide]
    high = band.astype(jnp.bfloat16)
    low = (band - high.astype(jnp.float32)).astype(jnp.bfloat16)
    first = first_ref[0]

    @pl.loop(0, length // block)
    def _(i):
        at = pl.multiple_of(lax.rem(first + i * block, length), block)
        start = pl.multiple_of(11 * cols + i * block, cols)
        for s in range(slots):
            window = mixed_ref[s, pl.ds(start, wide)]
            total = jnp.dot(high, window, preferred_element_type=jnp.float32)
            total += jnp.dot(low, window, preferred_element_type=jnp.float32)
            out_ref[s, pl.ds(at, block)] = total.astype(jnp.bfloat16)


def polar_filter(first, mixed, line, length):
    slots, _, channels = mixed.shape
    return pl.pallas_call(
        filter_kernel,
        out_shape=jax.ShapeDtypeStruct((slots, length, channels), jnp.bfloat16),
        in_specs=[smem(), vmem(), vmem()],
        out_specs=vmem(),
    )(first, mixed, line)


def body(field, land_mask, taps, gain, up, down, polar_rows, polar_owner, polar_taps):
    owners = lax.axis_size("lon")
    slots = 2
    gain = gain[None, :]
    coded, outgoing = prepare(field, land_mask, polar_rows, polar_owner, owners, slots)
    mixed_field, mixed = exchange(coded, outgoing, taps, gain, up, down)
    cols = field.shape[1]
    half = polar_taps.shape[0] // 2
    line = jnp.zeros((1, 256), jnp.float32)
    line = lax.dynamic_update_slice(line, polar_taps[None, :], (0, cols - half))
    length = owners * cols
    place = lax.div(lax.axis_index("lon"), 8) * 8 + 12 + (owners // 2 if NEAR_FIRST else 0)
    first = (lax.rem(place, owners) * cols)[None]
    polar_field = polar_filter(first, mixed, line, length)
    return (mixed_field, polar_field)


def solution(mesh):
    in_specs = (P("lat", "lon", None), P("lat", "lon"), P(), P(), P(), P(), P("lat"), P("lat"), P())
    out_specs = (P("lat", "lon", None), P(("lat", "lon"), None, None))
    return jax.shard_map(body, mesh=mesh, in_specs=in_specs, out_specs=out_specs, check_vma=False)
```

```python
import jax
import jax.numpy as jnp
from jax import lax
from jax.experimental import pallas as pl
from jax.experimental.pallas import tpu as pltpu
from jax.sharding import PartitionSpec as P

MESH = pl.DeviceIdType.MESH
DILATION = 4
LAND = 64.0
GELU_A = 0.7978845608028654
GELU_B = 0.044715 * GELU_A
GROUP = 8
CHUNK = 4
SLOTS = 2


def mix(tiles, land, keep, taps, gain, half_up, down):
    rows, _, _, channels = tiles.shape
    turned = pltpu.roll(tiles.reshape(rows * (keep + 8), 8, channels), 4, 1).reshape(tiles.shape)
    first_half = lax.broadcasted_iota(jnp.int32, (rows, keep + 7, 8, channels), 2) < 4
    halves = jnp.where(first_half, turned[:, :-1], turned[:, 1:])
    zonal = None
    for k in range(taps.shape[0]):
        start = (k - 7) * DILATION + 32
        source = halves if start % 8 else tiles
        term = taps[k][None, None, None, :] * source[:, start // 8 : start // 8 + keep]
        zonal = term if zonal is None else zonal + term
    zonal = zonal.reshape(rows * keep * 8, channels)
    centred = zonal - jnp.mean(zonal, axis=-1, keepdims=True)
    variance = jnp.mean(centred * centred, axis=-1, keepdims=True)
    normed = (centred * lax.rsqrt(variance + 1e-06) * gain).astype(jnp.bfloat16)
    half = jnp.dot(normed, half_up, preferred_element_type=jnp.float32).astype(jnp.bfloat16)
    bend = half * (jnp.bfloat16(2 * GELU_A) + jnp.bfloat16(8 * GELU_B) * (half * half))
    hidden = half + half * jnp.tanh(bend)
    branch = jnp.dot(hidden, down, preferred_element_type=jnp.float32)
    mixed = tiles[:, 4 : 4 + keep].reshape(-1, channels) + branch
    return jnp.where(land.reshape(-1, channels), 0.0, mixed).astype(jnp.bfloat16)


def layer_kernel(
    table_ref,
    filter_ref,
    field_hbm,
    mask_hbm,
    taps_hbm,
    gain_hbm,
    up_hbm,
    down_hbm,
    out_hbm,
    polar_hbm,
    field,
    mask,
    taps,
    gain,
    up,
    down,
    coded,
    masked,
    left,
    right,
    outgoing,
    pieces,
    mixed,
    out,
    polar,
    load_sem,
    store_sem,
    send_sem,
    piece_sem,
    halo_sem,
):
    lat_rows, cols, channels = field.shape
    owners = outgoing.shape[0]
    groups = owners // GROUP
    middle = groups // 2
    band = lax.axis_index("lat")
    me = lax.axis_index("lon")
    mine, low = lax.div(me, GROUP), lax.rem(me, GROUP)
    ahead, behind = lax.rem(me + 1, owners), lax.rem(me + owners - 1, owners)

    loads = [
        pltpu.make_async_copy(source, target, load_sem.at[k])
        for k, (source, target) in enumerate(
            [
                (field_hbm, field),
                (mask_hbm, mask),
                (taps_hbm, taps),
                (gain_hbm, gain),
                (up_hbm, up),
                (down_hbm, down),
            ]
        )
    ]
    for load in loads:
        load.start()
    barrier = pltpu.get_barrier_semaphore()

    @pl.loop(1, owners)
    def _(i):
        pl.semaphore_signal(
            barrier,
            inc=1,
            device_id=(band, lax.rem(me + i, owners)),
            device_id_type=MESH,
        )

    def span(tile, tiles):
        return pl.ds(pl.multiple_of(tile * cols, cols), tiles * cols)

    def piece_copy(position, other):
        relative = lax.rem(position + middle, groups)
        target = lax.rem(mine - relative + groups, groups) * GROUP + lax.rem(low + other, GROUP)
        return pltpu.make_async_remote_copy(
            src_ref=outgoing.at[target],
            dst_ref=pieces.at[:, span(position * GROUP + low, 1)],
            send_sem=send_sem.at[0],
            recv_sem=piece_sem.at[position],
            device_id=(band, target),
            device_id_type=MESH,
        )

    def halo_copy(side, target, k):
        return pltpu.make_async_remote_copy(
            src_ref=masked,
            dst_ref=side,
            send_sem=send_sem.at[1 + k],
            recv_sem=halo_sem.at[k],
            device_id=(band, target),
            device_id_type=MESH,
        )

    loads[0].wait()
    loads[1].wait()
    for r in range(lat_rows):
        wet = jnp.broadcast_to(mask[:, r : r + 1], (cols, channels)) != 0
        values = field[r].astype(jnp.float32)
        coded[r] = jnp.where(wet, values, LAND).astype(jnp.bfloat16)
        masked[r] = jnp.where(wet, values, 0.0).astype(jnp.bfloat16)
    coded[lat_rows] = jnp.full((cols, channels), LAND, jnp.bfloat16)

    @pl.loop(0, owners // 4)
    def _(i):
        for j in range(4):
            for s in range(SLOTS):
                outgoing[i * 4 + j, s] = coded[table_ref[s * owners + i * 4 + j]]

    pieces[:, span(middle * GROUP + low, 1)] = outgoing[me]
    for load in loads[2:]:
        load.wait()
    half_up = (up[...].astype(jnp.float32) * 0.5).astype(jnp.bfloat16)
    up[...] = half_up

    pl.semaphore_wait(barrier, owners - 1)
    to_ahead = halo_copy(left, ahead, 0)
    to_behind = halo_copy(right, behind, 1)

    def send(position):
        @pl.loop(1 if position == middle else 0, GROUP)
        def _(other):
            piece_copy(position, other).start()

    send(middle)
    for q in range(1, middle):
        if q == middle - 1:
            to_ahead.start()
            to_behind.start()
        send(middle - q)
        send(middle + q)
    send(groups)

    def arrived(position, tiles):
        landed = pieces.at[:, span(position * GROUP, tiles)]
        pltpu.make_async_copy(landed, landed, piece_sem.at[position]).wait()

    def mix_chunk(tile):
        keep = CHUNK * cols // 8
        tiles = pieces[:, span(tile - 1, CHUNK + 2)].astype(jnp.float32)
        tiles = tiles.reshape(SLOTS, keep + 8, 8, channels)
        land = tiles == LAND
        tiles = jnp.where(land, 0.0, tiles)
        result = mix(tiles, land[:, 4 : 4 + keep], keep, taps, gain[...], up[...], down[...])
        mixed[:, span(tile, CHUNK)] = result.reshape(SLOTS, CHUNK * cols, channels)

    arrived(middle, GROUP - 1)
    mix_chunk(middle * GROUP + 2)
    step = 8
    store_own = pltpu.make_async_copy(out, out_hbm, store_sem.at[0])

    @pl.loop(1, middle)
    def _(q):
        @pl.when(q == middle - 1)
        def _():
            to_ahead.wait_recv()
            to_behind.wait_recv()

            @pl.loop(0, lat_rows // step)
            def _(i):
                rows = pl.ds(i * step, step)
                tiles = jnp.concatenate(
                    [
                        ref[rows].astype(jnp.float32).reshape(step, cols // 8, 8, channels)
                        for ref in (left, masked, right)
                    ],
                    axis=1,
                )
                keep = cols // 8
                land = coded[rows].astype(jnp.float32).reshape(step, keep, 8, channels) == LAND
                result = mix(tiles, land, keep, taps, gain[...], up[...], down[...])
                out[rows] = result.reshape(step, cols, channels)

            store_own.start()

        arrived(middle - q, GROUP)
        arrived(middle + q, GROUP)

        @pl.loop(0, 4)
        def _(k):
            side = lax.div(k, 2)
            first = side * (middle * GROUP + 6 + (q - 1) * GROUP)
            first += (1 - side) * (middle * GROUP + 2 - q * GROUP)
            mix_chunk(first + lax.rem(k, 2) * CHUNK)

    block = CHUNK * cols
    wide = block + 2 * cols
    lane = lax.broadcasted_iota(jnp.int32, (1, 256), 1)
    line = jnp.zeros((1, 256), jnp.float32)
    for k in range(filter_ref.shape[0]):
        line = jnp.where(lane == k + cols - filter_ref.shape[0] // 2, filter_ref[k], line)
    weights = pltpu.roll(jnp.broadcast_to(line, (block, 256)), 0, 1, stride=1, stride_axis=0)
    weights = weights[:, :wide]
    high = weights.astype(jnp.bfloat16)
    rest = (weights - high.astype(jnp.float32)).astype(jnp.bfloat16)
    place = mine * GROUP + middle * GROUP + 12

    def store_block(i):
        at = pl.multiple_of(lax.rem(place + i * CHUNK, owners) * cols, block)
        return pltpu.make_async_copy(
            polar.at[:, span(i * CHUNK, CHUNK)], polar_hbm.at[:, pl.ds(at, block)], store_sem.at[1]
        )

    def filter_blocks(begin, end):
        @pl.loop(begin, end)
        def _(i):
            window = mixed[:, span(11 + i * CHUNK, CHUNK + 2)]
            window = jnp.concatenate([window[s] for s in range(SLOTS)], axis=1)
            total = jnp.dot(high, window, preferred_element_type=jnp.float32)
            total += jnp.dot(rest, window, preferred_element_type=jnp.float32)
            total = total.astype(jnp.bfloat16)
            for s in range(SLOTS):
                polar[s, span(i * CHUNK, CHUNK)] = total[:, s * channels : (s + 1) * channels]
            store_block(i).start()

    blocks = owners // CHUNK
    filter_blocks(0, blocks - 4)
    arrived(groups, GROUP)
    pieces[:, span(GROUP + owners, 3)] = pieces[:, span(GROUP, 3)]

    @pl.loop(0, 3)
    def _(k):
        mix_chunk(GROUP + owners - 10 + k * CHUNK)

    mixed[:, span(owners + 10, 3)] = mixed[:, span(10, 3)]
    filter_blocks(blocks - 4, blocks)

    to_ahead.wait_send()
    to_behind.wait_send()
    sent = outgoing.at[pl.ds(0, owners - 1)]
    pltpu.make_async_copy(sent, sent, send_sem.at[0]).wait()
    store_own.wait()
    pltpu.make_async_copy(polar, polar_hbm, store_sem.at[1]).wait()


def layer(table, polar_taps, field, mask, taps, gain, up, down, owners):
    lat_rows, cols, channels = field.shape
    length = owners * cols
    smem = pl.BlockSpec(memory_space=pltpu.SMEM)
    anywhere = pl.BlockSpec(memory_space=pl.ANY)
    tile = pltpu.VMEM(field.shape, jnp.bfloat16)
    operands = (field, mask, taps, gain, up, down)
    return pl.pallas_call(
        layer_kernel,
        out_shape=(
            jax.ShapeDtypeStruct(field.shape, jnp.bfloat16),
            jax.ShapeDtypeStruct((SLOTS, length, channels), jnp.bfloat16),
        ),
        in_specs=[smem] * 2 + [anywhere] * 6,
        out_specs=(anywhere, anywhere),
        scratch_shapes=[pltpu.VMEM(x.shape, x.dtype) for x in operands]
        + [
            pltpu.VMEM((lat_rows + 1, cols, channels), jnp.bfloat16),
            tile,
            tile,
            tile,
            pltpu.VMEM((owners, SLOTS, cols, channels), jnp.bfloat16),
            pltpu.VMEM((SLOTS, length + 11 * cols, channels), jnp.bfloat16),
            pltpu.VMEM((SLOTS, length + 13 * cols, channels), jnp.bfloat16),
            tile,
            pltpu.VMEM((SLOTS, length, channels), jnp.bfloat16),
            pltpu.SemaphoreType.DMA((len(operands),)),
            pltpu.SemaphoreType.DMA((2,)),
            pltpu.SemaphoreType.DMA((3,)),
            pltpu.SemaphoreType.DMA((9,)),
            pltpu.SemaphoreType.DMA((2,)),
        ],
        compiler_params=pltpu.CompilerParams(collective_id=0, has_side_effects=True),
    )(table, polar_taps, *operands)


def row_table(polar_rows, polar_owner, owners, none):
    entries = jnp.arange(polar_rows.shape[0], dtype=jnp.int32)
    same = (polar_owner[:, None] == polar_owner[None, :]) & (entries[None, :] < entries[:, None])
    rank = jnp.sum(same.astype(jnp.int32), axis=1)
    place = rank * owners + polar_owner
    places = jnp.arange(SLOTS * owners, dtype=jnp.int32)
    hit = place[None, :] == places[:, None]
    return none + jnp.sum(jnp.where(hit, polar_rows[None, :] - none, 0), axis=1)


def body(field, land_mask, taps, gain, up, down, polar_rows, polar_owner, polar_taps):
    owners = lax.axis_size("lon")
    table = row_table(polar_rows, polar_owner, owners, field.shape[0])
    return layer(table, polar_taps, field, land_mask.T, taps, gain[None, :], up, down, owners)


def solution(mesh):
    in_specs = (P("lat", "lon", None), P("lat", "lon"), P(), P(), P(), P(), P("lat"), P("lat"), P())
    out_specs = (P("lat", "lon", None), P(("lat", "lon"), None, None))
    return jax.shard_map(body, mesh=mesh, in_specs=in_specs, out_specs=out_specs, check_vma=False)
```

```python
import jax
import jax.numpy as jnp
from jax import lax
from jax.experimental import pallas as pl
from jax.experimental.pallas import tpu as pltpu
from jax.sharding import PartitionSpec as P

MESH = pl.DeviceIdType.MESH
DILATION = 4
LAND = 64.0
GELU_A = 0.7978845608028654
GELU_B = 0.044715 * GELU_A
GROUP = 8
CHUNK = 4
SLOTS = 2


def mix(tiles, land, keep, taps, gain, half_up, down):
    rows, _, _, channels = tiles.shape
    turned = pltpu.roll(tiles.reshape(rows * (keep + 8), 8, channels), 4, 1).reshape(tiles.shape)
    first_half = lax.broadcasted_iota(jnp.int32, (rows, keep + 7, 8, channels), 2) < 4
    halves = jnp.where(first_half, turned[:, :-1], turned[:, 1:])
    zonal = None
    for k in range(taps.shape[0]):
        start = (k - 7) * DILATION + 32
        source = halves if start % 8 else tiles
        term = taps[k][None, None, None, :] * source[:, start // 8 : start // 8 + keep]
        zonal = term if zonal is None else zonal + term
    zonal = zonal.reshape(rows * keep * 8, channels)
    centred = zonal - jnp.mean(zonal, axis=-1, keepdims=True)
    variance = jnp.mean(centred * centred, axis=-1, keepdims=True)
    normed = (centred * lax.rsqrt(variance + 1e-06) * gain).astype(jnp.bfloat16)
    half = jnp.dot(normed, half_up, preferred_element_type=jnp.float32)
    bend = half * (2 * GELU_A + 8 * GELU_B * (half * half))
    hidden = (half + half * jnp.tanh(bend)).astype(jnp.bfloat16)
    branch = jnp.dot(hidden, down, preferred_element_type=jnp.float32).astype(jnp.bfloat16)
    mixed = tiles[:, 4 : 4 + keep].reshape(-1, channels) + branch.astype(jnp.float32)
    return jnp.where(land.reshape(-1, channels), 0.0, mixed).astype(jnp.bfloat16)


def layer_kernel(
    rows_hbm,
    owner_hbm,
    filter_hbm,
    field_hbm,
    mask_hbm,
    taps_hbm,
    gain_hbm,
    up_hbm,
    down_hbm,
    out_result,
    polar_result,
    listed,
    owner,
    filter_ref,
    field,
    mask,
    taps,
    gain,
    up,
    down,
    table,
    table_ref,
    coded,
    masked,
    left,
    right,
    outgoing,
    pieces,
    mixed,
    out,
    polar,
    load_sem,
    store_sem,
    send_sem,
    piece_sem,
    halo_sem,
):
    lat_rows, cols, channels = field.shape
    owners = outgoing.shape[0]
    groups = owners // GROUP
    middle = groups // 2
    band = lax.axis_index("lat")
    me = lax.axis_index("lon")
    mine, low = lax.div(me, GROUP), lax.rem(me, GROUP)
    ahead, behind = lax.rem(me + 1, owners), lax.rem(me + owners - 1, owners)

    loads = [
        pltpu.make_async_copy(source, target, load_sem.at[k])
        for k, (source, target) in enumerate(
            [
                (rows_hbm, listed),
                (owner_hbm, owner),
                (mask_hbm, mask),
                (field_hbm, field),
                (filter_hbm, filter_ref),
                (taps_hbm, taps),
                (gain_hbm, gain),
                (up_hbm, up),
                (down_hbm, down),
            ]
        )
    ]
    barrier = pltpu.get_barrier_semaphore()

    @pl.loop(0, owners // 7)
    def _(i):
        for j in range(7):
            other = lax.rem(me + owners // 2 + 1 + i * 7 + j, owners)
            other = lax.rem(other + jnp.where(other == me, owners // 2, 0), owners)
            pl.semaphore_signal(barrier, inc=1, device_id=(band, other), device_id_type=MESH)

    for load in loads:
        load.start()

    def span(tile, tiles):
        return pl.ds(pl.multiple_of(tile * cols, cols), tiles * cols)

    def piece_copy(position, other):
        relative = lax.rem(position + middle, groups)
        target = lax.rem(mine - relative + groups, groups) * GROUP + lax.rem(low + other, GROUP)
        return pltpu.make_async_remote_copy(
            src_ref=outgoing.at[target],
            dst_ref=pieces.at[:, span(position * GROUP + low, 1)],
            send_sem=send_sem.at[0],
            recv_sem=piece_sem.at[position],
            device_id=(band, target),
            device_id_type=MESH,
        )

    def halo_copy(side, target, k):
        return pltpu.make_async_remote_copy(
            src_ref=masked,
            dst_ref=side,
            send_sem=send_sem.at[1 + k],
            recv_sem=halo_sem.at[k],
            device_id=(band, target),
            device_id_type=MESH,
        )

    loads[0].wait()
    loads[1].wait()
    entries = listed.shape[1]
    shape = (entries, entries)
    entry, earlier = (lax.broadcasted_iota(jnp.int32, shape, k) for k in range(2))
    owners_along = jnp.broadcast_to(owner[...], shape).astype(jnp.float32)
    rows_along = jnp.broadcast_to(listed[...], shape).astype(jnp.float32)

    def total(keep, values):
        return jnp.sum(jnp.where(keep, values, 0.0), axis=1, keepdims=True)

    owner_of = total(entry == earlier, owners_along)
    row_of = total(entry == earlier, rows_along).astype(jnp.int32)
    rank = total((owners_along == owner_of) & (earlier < entry), jnp.ones(shape, jnp.float32))
    place_of = (rank * owners + owner_of).astype(jnp.int32)
    slot = lax.broadcasted_iota(jnp.int32, (entries, SLOTS * owners), 1)
    fill = jnp.where(place_of == slot, row_of - lat_rows, 0)
    table[...] = lat_rows + jnp.sum(fill, axis=0, keepdims=True)
    to_scalars = pltpu.make_async_copy(table, table_ref, store_sem.at[0])
    to_scalars.start()
    loads[2].wait()
    loads[3].wait()
    for r in range(lat_rows):
        wet = jnp.broadcast_to(mask[:, r : r + 1], (cols, channels)) != 0
        values = field[r].astype(jnp.float32)
        coded[r] = jnp.where(wet, values, LAND).astype(jnp.bfloat16)
        masked[r] = jnp.where(wet, values, 0.0).astype(jnp.bfloat16)
    coded[lat_rows] = jnp.full((cols, channels), LAND, jnp.bfloat16)

    to_scalars.wait()

    @pl.loop(0, owners // 4)
    def _(i):
        for j in range(4):
            for s in range(SLOTS):
                outgoing[i * 4 + j, s] = coded[table_ref[0, s * owners + i * 4 + j]]

    pieces[:, span(middle * GROUP + low, 1)] = outgoing[me]
    for load in loads[4:]:
        load.wait()
    half_up = (up[...].astype(jnp.float32) * 0.5).astype(jnp.bfloat16)
    up[...] = half_up

    pl.semaphore_wait(barrier, owners - 1)
    to_ahead = halo_copy(left, ahead, 0)
    to_behind = halo_copy(right, behind, 1)

    def send(position):
        @pl.loop(1 if position == middle else 0, GROUP)
        def _(other):
            piece_copy(position, other).start()

    send(middle)
    for q in range(1, middle):
        if q == middle - 1:
            to_ahead.start()
            to_behind.start()
        send(middle - q)
        send(middle + q)
    send(groups)

    def arrived(position, tiles):
        landed = pieces.at[:, span(position * GROUP, tiles)]
        pltpu.make_async_copy(landed, landed, piece_sem.at[position]).wait()

    def mix_chunk(tile, tiles_wide):
        keep = tiles_wide * cols // 8
        tiles = pieces[:, span(tile - 1, tiles_wide + 2)].astype(jnp.float32)
        tiles = tiles.reshape(SLOTS, keep + 8, 8, channels)
        land = tiles == LAND
        tiles = jnp.where(land, 0.0, tiles)
        result = mix(tiles, land[:, 4 : 4 + keep], keep, taps, gain[...], up[...], down[...])
        mixed[:, span(tile, tiles_wide)] = result.reshape(SLOTS, tiles_wide * cols, channels)

    arrived(middle, GROUP - 1)
    mix_chunk(middle * GROUP + 2, 4)
    step = 16
    store_own = pltpu.make_async_copy(out, out_result, store_sem.at[0])

    @pl.loop(1, middle)
    def _(q):
        @pl.when(q == middle - 1)
        def _():
            to_ahead.wait_recv()
            to_behind.wait_recv()

            @pl.loop(0, lat_rows // step)
            def _(i):
                rows = pl.ds(i * step, step)
                tiles = jnp.concatenate(
                    [
                        ref[rows].astype(jnp.float32).reshape(step, cols // 8, 8, channels)
                        for ref in (left, masked, right)
                    ],
                    axis=1,
                )
                keep = cols // 8
                land = coded[rows].astype(jnp.float32).reshape(step, keep, 8, channels) == LAND
                result = mix(tiles, land, keep, taps, gain[...], up[...], down[...])
                out[rows] = result.reshape(step, cols, channels)

            store_own.start()

        arrived(middle - q, GROUP)
        arrived(middle + q, GROUP)

        @pl.loop(0, 2)
        def _(side):
            first = side * (middle * GROUP + 6 + (q - 1) * GROUP)
            first += (1 - side) * (middle * GROUP + 2 - q * GROUP)
            mix_chunk(first, GROUP)

    block = CHUNK * cols
    wide = block + 2 * cols
    lane = lax.broadcasted_iota(jnp.int32, (1, 256), 1)
    line = jnp.zeros((1, 256), jnp.float32)
    for k in range(filter_ref.shape[1]):
        line = jnp.where(lane == k + cols - filter_ref.shape[1] // 2, filter_ref[0, k], line)
    weights = pltpu.roll(jnp.broadcast_to(line, (block, 256)), 0, 1, stride=1, stride_axis=0)
    weights = weights[:, :wide]
    high = weights.astype(jnp.bfloat16)
    rest = (weights - high.astype(jnp.float32)).astype(jnp.bfloat16)
    place = mine * GROUP + middle * GROUP + 12

    def store_block(i):
        at = pl.multiple_of(lax.rem(place + i * CHUNK, owners) * cols, block)
        return pltpu.make_async_copy(
            polar.at[:, span(i * CHUNK, CHUNK)], polar_result.at[:, pl.ds(at, block)], store_sem.at[1]
        )

    def filter_blocks(begin, end):
        @pl.loop(begin, end)
        def _(i):
            window = mixed[:, span(11 + i * CHUNK, CHUNK + 2)]
            window = jnp.concatenate([window[s] for s in range(SLOTS)], axis=1)
            total = jnp.dot(high, window, preferred_element_type=jnp.float32)
            total += jnp.dot(rest, window, preferred_element_type=jnp.float32)
            total = total.astype(jnp.bfloat16)
            for s in range(SLOTS):
                polar[s, span(i * CHUNK, CHUNK)] = total[:, s * channels : (s + 1) * channels]
            store_block(i).start()

    blocks = owners // CHUNK
    filter_blocks(0, blocks - 4)
    arrived(groups, GROUP)
    pieces[:, span(GROUP + owners, 3)] = pieces[:, span(GROUP, 3)]

    mix_chunk(GROUP + owners - 10, 12)

    mixed[:, span(owners + 10, 3)] = mixed[:, span(10, 3)]
    filter_blocks(blocks - 4, blocks)

    to_ahead.wait_send()
    to_behind.wait_send()
    sent = outgoing.at[pl.ds(0, owners - 1)]
    pltpu.make_async_copy(sent, sent, send_sem.at[0]).wait()
    store_own.wait()
    pltpu.make_async_copy(polar, polar_result, store_sem.at[1]).wait()


def layer(polar_rows, polar_owner, polar_taps, field, mask, taps, gain, up, down, owners):
    lat_rows, cols, channels = field.shape
    length = owners * cols
    tile = pltpu.VMEM(field.shape, jnp.bfloat16)
    operands = (polar_rows, polar_owner, polar_taps, field, mask, taps, gain, up, down)
    held = [pltpu.VMEM(x.shape, x.dtype) for x in operands]
    held[2] = pltpu.SMEM(polar_taps.shape, polar_taps.dtype)
    return pl.pallas_call(
        layer_kernel,
        out_shape=(
            jax.ShapeDtypeStruct(field.shape, jnp.bfloat16),
            jax.ShapeDtypeStruct((SLOTS, length, channels), jnp.bfloat16),
        ),
        in_specs=[pl.BlockSpec(memory_space=pltpu.HBM)] * len(operands),
        out_specs=(pl.BlockSpec(memory_space=pl.ANY),) * 2,
        scratch_shapes=held
        + [
            pltpu.VMEM((1, SLOTS * owners), jnp.int32),
            pltpu.SMEM((1, SLOTS * owners), jnp.int32),
            pltpu.VMEM((lat_rows + 1, cols, channels), jnp.bfloat16),
            tile,
            tile,
            tile,
            pltpu.VMEM((owners, SLOTS, cols, channels), jnp.bfloat16),
            pltpu.VMEM((SLOTS, length + 11 * cols, channels), jnp.bfloat16),
            pltpu.VMEM((SLOTS, length + 13 * cols, channels), jnp.bfloat16),
            tile,
            pltpu.VMEM((SLOTS, length, channels), jnp.bfloat16),
            pltpu.SemaphoreType.DMA((len(operands),)),
            pltpu.SemaphoreType.DMA((2,)),
            pltpu.SemaphoreType.DMA((3,)),
            pltpu.SemaphoreType.DMA((9,)),
            pltpu.SemaphoreType.DMA((2,)),
        ],
        compiler_params=pltpu.CompilerParams(
            collective_id=0, has_side_effects=True, vmem_limit_bytes=32 << 20
        ),
    )(*(pltpu.with_memory_space_constraint(x, pltpu.HBM) for x in operands))


def write_kernel(field_ref, polar_ref, field_out, polar_out, sem):
    copies = [
        pltpu.make_async_copy(polar_ref, polar_out, sem.at[0]),
        pltpu.make_async_copy(field_ref, field_out, sem.at[1]),
    ]
    for copy in copies:
        copy.start()
    for copy in copies:
        copy.wait()


def write(mixed_field, polar_field):
    return pl.pallas_call(
        write_kernel,
        out_shape=tuple(jax.ShapeDtypeStruct(x.shape, x.dtype) for x in (mixed_field, polar_field)),
        in_specs=[pl.BlockSpec(memory_space=pl.ANY)] * 2,
        out_specs=(pl.BlockSpec(memory_space=pltpu.HBM),) * 2,
        scratch_shapes=[pltpu.SemaphoreType.DMA((2,))],
        compiler_params=pltpu.CompilerParams(vmem_limit_bytes=1 << 20),
    )(mixed_field, polar_field)


def body(field, land_mask, taps, gain, up, down, polar_rows, polar_owner, polar_taps):
    owners = lax.axis_size("lon")
    lists = (polar_rows[None, :], polar_owner[None, :], polar_taps[None, :])
    return write(*layer(*lists, field, land_mask.T, taps, gain[None, :], up, down, owners))


def solution(mesh):
    in_specs = (P("lat", "lon", None), P("lat", "lon"), P(), P(), P(), P(), P("lat"), P("lat"), P())
    out_specs = (P("lat", "lon", None), P(("lat", "lon"), None, None))
    return jax.shard_map(body, mesh=mesh, in_specs=in_specs, out_specs=out_specs, check_vma=False)
```

```python
import jax
import jax.numpy as jnp
from jax import lax
from jax.experimental import pallas as pl
from jax.experimental.pallas import tpu as pltpu
from jax.sharding import PartitionSpec as P

MESH = pl.DeviceIdType.MESH
DILATION = 4
LAND = 64.0
GELU_A = 0.7978845608028654
GELU_B = 0.044715 * GELU_A
GROUP = 8
CHUNK = 4
SLOTS = 2


def mix(tiles, land, keep, taps, gain, half_up, down):
    rows, _, _, channels = tiles.shape
    turned = pltpu.roll(tiles.reshape(rows * (keep + 8), 8, channels), 4, 1).reshape(tiles.shape)
    first_half = lax.broadcasted_iota(jnp.int32, (rows, keep + 7, 8, channels), 2) < 4
    halves = jnp.where(first_half, turned[:, :-1], turned[:, 1:])
    zonal = None
    for k in range(taps.shape[0]):
        start = (k - 7) * DILATION + 32
        source = halves if start % 8 else tiles
        term = taps[k][None, None, None, :] * source[:, start // 8 : start // 8 + keep]
        zonal = term if zonal is None else zonal + term
    zonal = zonal.reshape(rows * keep * 8, channels)
    centred = zonal - jnp.mean(zonal, axis=-1, keepdims=True)
    variance = jnp.mean(centred * centred, axis=-1, keepdims=True)
    normed = (centred * lax.rsqrt(variance + 1e-06) * gain).astype(jnp.bfloat16)
    half = jnp.dot(normed, half_up, preferred_element_type=jnp.float32)
    bend = half * (2 * GELU_A + 8 * GELU_B * (half * half))
    hidden = (half + half * jnp.tanh(bend)).astype(jnp.bfloat16)
    branch = jnp.dot(hidden, down, preferred_element_type=jnp.float32).astype(jnp.bfloat16)
    mixed = tiles[:, 4 : 4 + keep].reshape(-1, channels) + branch.astype(jnp.float32)
    return jnp.where(land.reshape(-1, channels), 0.0, mixed).astype(jnp.bfloat16)


def layer_kernel(
    rows_hbm,
    owner_hbm,
    filter_hbm,
    field_hbm,
    mask_hbm,
    taps_hbm,
    gain_hbm,
    up_hbm,
    down_hbm,
    out_result,
    polar_result,
    listed,
    owner,
    filter_ref,
    field,
    mask,
    taps,
    gain,
    up,
    down,
    table,
    table_ref,
    coded,
    masked,
    left,
    right,
    passing,
    outgoing,
    pieces,
    mixed,
    out,
    polar,
    load_sem,
    store_sem,
    send_sem,
    piece_sem,
    halo_sem,
):
    lat_rows, cols, channels = field.shape
    owners = outgoing.shape[0]
    groups = owners // GROUP
    middle = groups // 2
    band = lax.axis_index("lat")
    me = lax.axis_index("lon")
    mine, low = lax.div(me, GROUP), lax.rem(me, GROUP)
    ahead, behind = lax.rem(me + 1, owners), lax.rem(me + owners - 1, owners)

    loads = [
        pltpu.make_async_copy(source, target, load_sem.at[k])
        for k, (source, target) in enumerate(
            [
                (rows_hbm, listed),
                (owner_hbm, owner),
                (mask_hbm, mask),
                (field_hbm, field),
                (filter_hbm, filter_ref),
                (taps_hbm, taps),
                (gain_hbm, gain),
                (up_hbm, up),
                (down_hbm, down),
            ]
        )
    ]
    barrier = pltpu.get_barrier_semaphore()

    @pl.loop(0, owners // 7)
    def _(i):
        for j in range(7):
            other = lax.rem(me + owners // 2 + 1 + i * 7 + j, owners)
            other = lax.rem(other + jnp.where(other == me, owners // 2, 0), owners)
            pl.semaphore_signal(barrier, inc=1, device_id=(band, other), device_id_type=MESH)

    for load in loads:
        load.start()

    def span(tile, tiles):
        return pl.ds(pl.multiple_of(tile * cols, cols), tiles * cols)

    def piece_copy(position, other):
        relative = lax.rem(position + middle, groups)
        target = lax.rem(mine - relative + groups, groups) * GROUP + lax.rem(low + other, GROUP)
        return pltpu.make_async_remote_copy(
            src_ref=outgoing.at[target],
            dst_ref=pieces.at[:, span(position * GROUP + low, 1)],
            send_sem=send_sem.at[0],
            recv_sem=piece_sem.at[position],
            device_id=(band, target),
            device_id_type=MESH,
        )

    def halo_copy(side, target, k):
        return pltpu.make_async_remote_copy(
            src_ref=masked,
            dst_ref=side,
            send_sem=send_sem.at[1 + k],
            recv_sem=halo_sem.at[k],
            device_id=(band, target),
            device_id_type=MESH,
        )

    loads[0].wait()
    loads[1].wait()
    entries = listed.shape[1]
    shape = (entries, entries)
    entry, earlier = (lax.broadcasted_iota(jnp.int32, shape, k) for k in range(2))
    owners_along = jnp.broadcast_to(owner[...], shape).astype(jnp.float32)
    rows_along = jnp.broadcast_to(listed[...], shape).astype(jnp.float32)

    def total(keep, values):
        return jnp.sum(jnp.where(keep, values, 0.0), axis=1, keepdims=True)

    owner_of = total(entry == earlier, owners_along)
    row_of = total(entry == earlier, rows_along).astype(jnp.int32)
    rank = total((owners_along == owner_of) & (earlier < entry), jnp.ones(shape, jnp.float32))
    place_of = (rank * owners + owner_of).astype(jnp.int32)
    slot = lax.broadcasted_iota(jnp.int32, (entries, SLOTS * owners), 1)
    fill = jnp.where(place_of == slot, row_of - lat_rows, 0)
    table[...] = lat_rows + jnp.sum(fill, axis=0, keepdims=True)
    to_scalars = pltpu.make_async_copy(table, table_ref, store_sem.at[0])
    to_scalars.start()
    loads[2].wait()
    loads[3].wait()
    for r in range(lat_rows):
        wet = jnp.broadcast_to(mask[:, r : r + 1], (cols, channels)) != 0
        values = field[r].astype(jnp.float32)
        coded[r] = jnp.where(wet, values, LAND).astype(jnp.bfloat16)
        masked[r] = jnp.where(wet, values, 0.0).astype(jnp.bfloat16)
    coded[lat_rows] = jnp.full((cols, channels), LAND, jnp.bfloat16)

    to_scalars.wait()

    @pl.loop(0, owners // 4)
    def _(i):
        for j in range(4):
            for s in range(SLOTS):
                outgoing[i * 4 + j, s] = coded[table_ref[0, s * owners + i * 4 + j]]

    pieces[:, span(middle * GROUP + low, 1)] = outgoing[me]
    for load in loads[4:]:
        load.wait()
    half_up = (up[...].astype(jnp.float32) * 0.5).astype(jnp.bfloat16)
    up[...] = half_up

    pl.semaphore_wait(barrier, owners - 1)
    to_ahead = halo_copy(left, ahead, 0)
    to_behind = halo_copy(right, behind, 1)

    def send(position):
        @pl.loop(1 if position == middle else 0, GROUP)
        def _(other):
            piece_copy(position, other).start()

    parts = GROUP // 2
    quarter = lat_rows // parts
    column = lax.div(low, 2)

    def rows_of(k):
        return pl.ds(k * quarter, quarter)

    def quarter_copy(k, side, step, k_side):
        over = lax.rem(mine + step, groups) * GROUP
        direct = k == (parts - 1 if k_side == 0 else 0)
        target = over + (GROUP - 1 if k_side else 0) if direct else mine * GROUP + 2 * k + 1 - k_side
        return pltpu.make_async_remote_copy(
            src_ref=masked.at[rows_of(k)],
            dst_ref=side.at[rows_of(k)] if direct else passing,
            send_sem=send_sem.at[1 + k_side],
            recv_sem=halo_sem.at[k_side] if direct else halo_sem.at[2],
            device_id=(band, target),
            device_id_type=MESH,
        )

    def hand_on(side, k_side):
        return pltpu.make_async_remote_copy(
            src_ref=passing,
            dst_ref=side.at[rows_of(column)],
            send_sem=send_sem.at[3],
            recv_sem=halo_sem.at[k_side],
            device_id=(
                band,
                lax.rem(mine + (groups - 1 if k_side else 1), groups) * GROUP
                + (GROUP - 1 if k_side else 0),
            ),
            device_id_type=MESH,
        )

    first, final = low == 0, low == GROUP - 1
    inner, outer = low != 0, low != GROUP - 1
    odd = lax.rem(low, 2) == 1
    hands_left = odd & (low < GROUP - 1)
    hands_right = (lax.rem(low, 2) == 0) & (low > 0)
    pass_left, pass_right = hand_on(left, 0), hand_on(right, 1)

    @pl.when(final)
    def _():
        for k in range(parts):
            quarter_copy(k, left, 1, 0).start()

    @pl.when(first)
    def _():
        for k in range(parts):
            quarter_copy(k, right, groups - 1, 1).start()

    send(middle)
    for q in (1, 2):
        send(middle - q)
        send(middle + q)

    @pl.when(hands_left | hands_right)
    def _():
        pltpu.make_async_copy(passing, passing, halo_sem.at[2]).wait()

    pl.when(hands_left)(pass_left.start)
    pl.when(hands_right)(pass_right.start)
    pl.when(outer)(to_ahead.start)
    pl.when(inner)(to_behind.start)
    for q in range(3, middle):
        send(middle - q)
        send(middle + q)
    send(groups)

    def arrived(position, tiles):
        landed = pieces.at[:, span(position * GROUP, tiles)]
        pltpu.make_async_copy(landed, landed, piece_sem.at[position]).wait()

    def mix_chunk(tile, tiles_wide, at=pl.ds(0, SLOTS)):
        keep = tiles_wide * cols // 8
        tiles = pieces[at, span(tile - 1, tiles_wide + 2)].astype(jnp.float32)
        tiles = tiles.reshape(at.size, keep + 8, 8, channels)
        land = tiles == LAND
        tiles = jnp.where(land, 0.0, tiles)
        result = mix(tiles, land[:, 4 : 4 + keep], keep, taps, gain[...], up[...], down[...])
        mixed[at, span(tile, tiles_wide)] = result.reshape(at.size, tiles_wide * cols, channels)

    arrived(middle, GROUP - 1)
    mix_chunk(middle * GROUP + 1, GROUP - 2)
    step = 16
    store_own = pltpu.make_async_copy(out, out_result, store_sem.at[0])

    @pl.loop(1, middle)
    def _(q):
        @pl.when(q == middle - 1)
        def _():
            to_ahead.wait_recv()
            to_behind.wait_recv()

            @pl.loop(0, lat_rows // step)
            def _(i):
                rows = pl.ds(i * step, step)
                tiles = jnp.concatenate(
                    [
                        ref[rows].astype(jnp.float32).reshape(step, cols // 8, 8, channels)
                        for ref in (left, masked, right)
                    ],
                    axis=1,
                )
                keep = cols // 8
                land = coded[rows].astype(jnp.float32).reshape(step, keep, 8, channels) == LAND
                result = mix(tiles, land, keep, taps, gain[...], up[...], down[...])
                out[rows] = result.reshape(step, cols, channels)

            store_own.start()

        arrived(middle - q, GROUP)
        arrived(middle + q, GROUP)

        @pl.loop(0, 2)
        def _(side):
            first = side * (middle * GROUP + 7 + (q - 1) * GROUP)
            first += (1 - side) * (middle * GROUP + 1 - q * GROUP)
            mix_chunk(first, GROUP)

    block = CHUNK * cols
    wide = block + 2 * cols
    lane = lax.broadcasted_iota(jnp.int32, (1, 256), 1)
    line = jnp.zeros((1, 256), jnp.float32)
    for k in range(filter_ref.shape[1]):
        line = jnp.where(lane == k + cols - filter_ref.shape[1] // 2, filter_ref[0, k], line)
    weights = pltpu.roll(jnp.broadcast_to(line, (block, 256)), 0, 1, stride=1, stride_axis=0)
    weights = weights[:, :wide]
    high = weights.astype(jnp.bfloat16)
    rest = (weights - high.astype(jnp.float32)).astype(jnp.bfloat16)
    place = mine * GROUP + middle * GROUP + 12

    def store_block(i, at):
        there = pl.multiple_of(lax.rem(place + i * CHUNK, owners) * cols, block)
        return pltpu.make_async_copy(
            polar.at[at, span(i * CHUNK, CHUNK)],
            polar_result.at[at, pl.ds(there, block)],
            store_sem.at[1],
        )

    def filtered(window):
        total = jnp.dot(high, window, preferred_element_type=jnp.float32)
        total += jnp.dot(rest, window, preferred_element_type=jnp.float32)
        return total.astype(jnp.bfloat16)

    blocks = owners // CHUNK
    both = pl.ds(0, SLOTS)
    pieces[:, span(GROUP + owners, 2)] = pieces[:, span(GROUP, 2)]
    mixed[:, span(owners + 9, 4)] = mixed[:, span(9, 4)]

    @pl.loop(0, blocks - 4)
    def _(i):
        window = mixed[:, span(11 + i * CHUNK, CHUNK + 2)]
        result = filtered(jnp.concatenate([window[s] for s in range(SLOTS)], axis=1))
        for s in range(SLOTS):
            polar[s, span(i * CHUNK, CHUNK)] = result[:, s * channels : (s + 1) * channels]
        store_block(i, both).start()

    arrived(groups, GROUP)
    mix_chunk(owners - 1, GROUP + 2)
    late = range(blocks - 4, blocks)
    windows = [mixed[:, span(11 + i * CHUNK, CHUNK + 2)] for i in late]
    windows = [window[s] for window in windows for s in range(SLOTS)]
    result = filtered(jnp.concatenate(windows, axis=1))
    for k, i in enumerate(late):
        for s in range(SLOTS):
            at = (k * SLOTS + s) * channels
            polar[s, span(i * CHUNK, CHUNK)] = result[:, at : at + channels]
    for i in late:
        store_block(i, both).start()

    to_ahead.wait_send()
    to_behind.wait_send()
    pl.when(hands_left)(pass_left.wait_send)
    pl.when(hands_right)(pass_right.wait_send)
    sent = outgoing.at[pl.ds(0, owners - 1)]
    pltpu.make_async_copy(sent, sent, send_sem.at[0]).wait()
    store_own.wait()
    pltpu.make_async_copy(polar, polar_result, store_sem.at[1]).wait()


def layer(polar_rows, polar_owner, polar_taps, field, mask, taps, gain, up, down, owners):
    lat_rows, cols, channels = field.shape
    length = owners * cols
    tile = pltpu.VMEM(field.shape, jnp.bfloat16)
    operands = (polar_rows, polar_owner, polar_taps, field, mask, taps, gain, up, down)
    held = [pltpu.VMEM(x.shape, x.dtype) for x in operands]
    held[2] = pltpu.SMEM(polar_taps.shape, polar_taps.dtype)
    return pl.pallas_call(
        layer_kernel,
        out_shape=(
            jax.ShapeDtypeStruct(field.shape, jnp.bfloat16),
            jax.ShapeDtypeStruct((SLOTS, length, channels), jnp.bfloat16),
        ),
        in_specs=[pl.BlockSpec(memory_space=pltpu.HBM)] * len(operands),
        out_specs=(pl.BlockSpec(memory_space=pl.ANY),) * 2,
        scratch_shapes=held
        + [
            pltpu.VMEM((1, SLOTS * owners), jnp.int32),
            pltpu.SMEM((1, SLOTS * owners), jnp.int32),
            pltpu.VMEM((lat_rows + 1, cols, channels), jnp.bfloat16),
            tile,
            tile,
            tile,
            pltpu.VMEM((lat_rows // (GROUP // 2), cols, channels), jnp.bfloat16),
            pltpu.VMEM((owners, SLOTS, cols, channels), jnp.bfloat16),
            pltpu.VMEM((SLOTS, length + 11 * cols, channels), jnp.bfloat16),
            pltpu.VMEM((SLOTS, length + 13 * cols, channels), jnp.bfloat16),
            tile,
            pltpu.VMEM((SLOTS, length, channels), jnp.bfloat16),
            pltpu.SemaphoreType.DMA((len(operands),)),
            pltpu.SemaphoreType.DMA((2,)),
            pltpu.SemaphoreType.DMA((4,)),
            pltpu.SemaphoreType.DMA((9,)),
            pltpu.SemaphoreType.DMA((3,)),
        ],
        compiler_params=pltpu.CompilerParams(
            collective_id=0, has_side_effects=True, vmem_limit_bytes=32 << 20
        ),
    )(*(pltpu.with_memory_space_constraint(x, pltpu.HBM) for x in operands))


def write_kernel(field_ref, polar_ref, field_out, polar_out, sem):
    parts = sem.shape[0] // 3
    wide, high = polar_ref.shape[1] // (2 * parts), field_ref.shape[0] // parts
    copies = []
    for k in range(2 * parts):
        at = pl.ds(k * wide, wide)
        copies.append(pltpu.make_async_copy(polar_ref.at[:, at], polar_out.at[:, at], sem.at[k]))
    for k in range(parts):
        at = pl.ds(k * high, high)
        copies.append(
            pltpu.make_async_copy(field_ref.at[at], field_out.at[at], sem.at[2 * parts + k])
        )
    for copy in copies:
        copy.start()
    for copy in copies:
        copy.wait()


def write(mixed_field, polar_field):
    return pl.pallas_call(
        write_kernel,
        out_shape=tuple(jax.ShapeDtypeStruct(x.shape, x.dtype) for x in (mixed_field, polar_field)),
        in_specs=[pl.BlockSpec(memory_space=pl.ANY)] * 2,
        out_specs=(pl.BlockSpec(memory_space=pltpu.HBM),) * 2,
        scratch_shapes=[pltpu.SemaphoreType.DMA((6,))],
        compiler_params=pltpu.CompilerParams(vmem_limit_bytes=1 << 20),
    )(mixed_field, polar_field)


def body(field, land_mask, taps, gain, up, down, polar_rows, polar_owner, polar_taps):
    owners = lax.axis_size("lon")
    lists = (polar_rows[None, :], polar_owner[None, :], polar_taps[None, :])
    return write(*layer(*lists, field, land_mask.T, taps, gain[None, :], up, down, owners))


def solution(mesh):
    in_specs = (P("lat", "lon", None), P("lat", "lon"), P(), P(), P(), P(), P("lat"), P("lat"), P())
    out_specs = (P("lat", "lon", None), P(("lat", "lon"), None, None))
    return jax.shard_map(body, mesh=mesh, in_specs=in_specs, out_specs=out_specs, check_vma=False)
```

```python
import jax
import jax.numpy as jnp
from jax import lax
from jax.experimental import pallas as pl
from jax.experimental.pallas import tpu as pltpu
from jax.sharding import PartitionSpec as P

MESH = pl.DeviceIdType.MESH
DILATION = 4
LAND = 64.0
GELU_A = 0.7978845608028654
GELU_B = 0.044715 * GELU_A
GROUP = 8
CHUNK = 4
SLOTS = 2


def mix(tiles, land, keep, taps, gain, half_up, down):
    rows, _, _, channels = tiles.shape
    turned = pltpu.roll(tiles.reshape(rows * (keep + 8), 8, channels), 4, 1).reshape(tiles.shape)
    first_half = lax.broadcasted_iota(jnp.int32, (rows, keep + 7, 8, channels), 2) < 4
    halves = jnp.where(first_half, turned[:, :-1], turned[:, 1:])
    zonal = None
    for k in range(taps.shape[0]):
        start = (k - 7) * DILATION + 32
        source = halves if start % 8 else tiles
        term = taps[k][None, None, None, :] * source[:, start // 8 : start // 8 + keep]
        zonal = term if zonal is None else zonal + term
    zonal = zonal.reshape(rows * keep * 8, channels)
    centred = zonal - jnp.mean(zonal, axis=-1, keepdims=True)
    variance = jnp.mean(centred * centred, axis=-1, keepdims=True)
    normed = (centred * lax.rsqrt(variance + 1e-06) * gain).astype(jnp.bfloat16)
    half = jnp.dot(normed, half_up, preferred_element_type=jnp.float32)
    bend = half * (2 * GELU_A + 8 * GELU_B * (half * half))
    hidden = (half + half * jnp.tanh(bend)).astype(jnp.bfloat16)
    branch = jnp.dot(hidden, down, preferred_element_type=jnp.float32).astype(jnp.bfloat16)
    mixed = tiles[:, 4 : 4 + keep].reshape(-1, channels) + branch.astype(jnp.float32)
    return jnp.where(land.reshape(-1, channels), 0.0, mixed).astype(jnp.bfloat16)


def layer_kernel(
    rows_hbm,
    owner_hbm,
    filter_hbm,
    field_hbm,
    mask_hbm,
    taps_hbm,
    gain_hbm,
    up_hbm,
    down_hbm,
    out_result,
    polar_result,
    listed,
    owner,
    filter_ref,
    field,
    mask,
    taps,
    gain,
    up,
    down,
    table,
    table_ref,
    coded,
    masked,
    left,
    right,
    passing,
    outgoing,
    pieces,
    mixed,
    load_sem,
    store_sem,
    send_sem,
    piece_sem,
    halo_sem,
):
    lat_rows, cols, channels = field.shape
    owners = outgoing.shape[0]
    groups = owners // GROUP
    middle = groups // 2
    band = lax.axis_index("lat")
    me = lax.axis_index("lon")
    mine, low = lax.div(me, GROUP), lax.rem(me, GROUP)
    ahead, behind = lax.rem(me + 1, owners), lax.rem(me + owners - 1, owners)

    loads = [
        pltpu.make_async_copy(source, target, load_sem.at[k])
        for k, (source, target) in enumerate(
            [
                (rows_hbm, listed),
                (owner_hbm, owner),
                (mask_hbm, mask),
                (field_hbm, field),
                (filter_hbm, filter_ref),
                (taps_hbm, taps),
                (gain_hbm, gain),
                (up_hbm, up),
                (down_hbm, down),
            ]
        )
    ]
    barrier = pltpu.get_barrier_semaphore()

    @pl.loop(0, owners // 7)
    def _(i):
        for j in range(7):
            other = lax.rem(me + owners // 2 + 1 + i * 7 + j, owners)
            other = lax.rem(other + jnp.where(other == me, owners // 2, 0), owners)
            pl.semaphore_signal(barrier, inc=1, device_id=(band, other), device_id_type=MESH)

    for load in loads:
        load.start()

    def span(tile, tiles):
        return pl.ds(pl.multiple_of(tile * cols, cols), tiles * cols)

    def piece_copy(position, other):
        relative = lax.rem(position + middle, groups)
        target = lax.rem(mine - relative + groups, groups) * GROUP + lax.rem(low + other, GROUP)
        return pltpu.make_async_remote_copy(
            src_ref=outgoing.at[target],
            dst_ref=pieces.at[:, span(position * GROUP + low, 1)],
            send_sem=send_sem.at[0],
            recv_sem=piece_sem.at[position],
            device_id=(band, target),
            device_id_type=MESH,
        )

    def halo_copy(side, target, k):
        return pltpu.make_async_remote_copy(
            src_ref=masked,
            dst_ref=side,
            send_sem=send_sem.at[1 + k],
            recv_sem=halo_sem.at[k],
            device_id=(band, target),
            device_id_type=MESH,
        )

    loads[0].wait()
    loads[1].wait()
    entries = listed.shape[1]
    shape = (entries, entries)
    entry, earlier = (lax.broadcasted_iota(jnp.int32, shape, k) for k in range(2))
    owners_along = jnp.broadcast_to(owner[...], shape).astype(jnp.float32)
    rows_along = jnp.broadcast_to(listed[...], shape).astype(jnp.float32)

    def total(keep, values):
        return jnp.sum(jnp.where(keep, values, 0.0), axis=1, keepdims=True)

    owner_of = total(entry == earlier, owners_along)
    row_of = total(entry == earlier, rows_along).astype(jnp.int32)
    rank = total((owners_along == owner_of) & (earlier < entry), jnp.ones(shape, jnp.float32))
    place_of = (rank * owners + owner_of).astype(jnp.int32)
    slot = lax.broadcasted_iota(jnp.int32, (entries, SLOTS * owners), 1)
    fill = jnp.where(place_of == slot, row_of - lat_rows, 0)
    table[...] = lat_rows + jnp.sum(fill, axis=0, keepdims=True)
    to_scalars = pltpu.make_async_copy(table, table_ref, store_sem.at[0])
    to_scalars.start()
    loads[2].wait()
    loads[3].wait()
    for r in range(lat_rows):
        wet = jnp.broadcast_to(mask[:, r : r + 1], (cols, channels)) != 0
        values = field[r].astype(jnp.float32)
        coded[r] = jnp.where(wet, values, LAND).astype(jnp.bfloat16)
        masked[r] = jnp.where(wet, values, 0.0).astype(jnp.bfloat16)
    coded[lat_rows] = jnp.full((cols, channels), LAND, jnp.bfloat16)

    to_scalars.wait()

    @pl.loop(0, owners // 4)
    def _(i):
        for j in range(4):
            for s in range(SLOTS):
                outgoing[i * 4 + j, s] = coded[table_ref[0, s * owners + i * 4 + j]]

    pieces[:, span(middle * GROUP + low, 1)] = outgoing[me]
    for load in loads[4:]:
        load.wait()
    half_up = (up[...].astype(jnp.float32) * 0.5).astype(jnp.bfloat16)
    up[...] = half_up

    pl.semaphore_wait(barrier, owners - 1)
    to_ahead = halo_copy(left, ahead, 0)
    to_behind = halo_copy(right, behind, 1)

    def send(position):
        @pl.loop(1 if position == middle else 0, GROUP)
        def _(other):
            piece_copy(position, other).start()

    parts = GROUP // 2
    quarter = lat_rows // parts
    column = lax.div(low, 2)

    def rows_of(k):
        return pl.ds(k * quarter, quarter)

    def quarter_copy(k, side, step, k_side):
        over = lax.rem(mine + step, groups) * GROUP
        direct = k == (parts - 1 if k_side == 0 else 0)
        target = over + (GROUP - 1 if k_side else 0) if direct else mine * GROUP + 2 * k + 1 - k_side
        return pltpu.make_async_remote_copy(
            src_ref=masked.at[rows_of(k)],
            dst_ref=side.at[rows_of(k)] if direct else passing,
            send_sem=send_sem.at[1 + k_side],
            recv_sem=halo_sem.at[k_side] if direct else halo_sem.at[2],
            device_id=(band, target),
            device_id_type=MESH,
        )

    def hand_on(side, k_side):
        return pltpu.make_async_remote_copy(
            src_ref=passing,
            dst_ref=side.at[rows_of(column)],
            send_sem=send_sem.at[3],
            recv_sem=halo_sem.at[k_side],
            device_id=(
                band,
                lax.rem(mine + (groups - 1 if k_side else 1), groups) * GROUP
                + (GROUP - 1 if k_side else 0),
            ),
            device_id_type=MESH,
        )

    first, final = low == 0, low == GROUP - 1
    inner, outer = low != 0, low != GROUP - 1
    odd = lax.rem(low, 2) == 1
    hands_left = odd & (low < GROUP - 1)
    hands_right = (lax.rem(low, 2) == 0) & (low > 0)
    pass_left, pass_right = hand_on(left, 0), hand_on(right, 1)

    @pl.when(final)
    def _():
        for k in range(parts):
            quarter_copy(k, left, 1, 0).start()

    @pl.when(first)
    def _():
        for k in range(parts):
            quarter_copy(k, right, groups - 1, 1).start()

    send(middle)
    for q in (1, 2):
        send(middle - q)
        send(middle + q)

    @pl.when(hands_left | hands_right)
    def _():
        pltpu.make_async_copy(passing, passing, halo_sem.at[2]).wait()

    pl.when(hands_left)(pass_left.start)
    pl.when(hands_right)(pass_right.start)
    pl.when(outer)(to_ahead.start)
    pl.when(inner)(to_behind.start)
    for q in range(3, middle):
        send(middle - q)
        send(middle + q)
    send(groups)

    def arrived(position, tiles):
        landed = pieces.at[:, span(position * GROUP, tiles)]
        pltpu.make_async_copy(landed, landed, piece_sem.at[position]).wait()

    def mix_chunk(tile, tiles_wide, at=pl.ds(0, SLOTS)):
        keep = tiles_wide * cols // 8
        tiles = pieces[at, span(tile - 1, tiles_wide + 2)].astype(jnp.float32)
        tiles = tiles.reshape(at.size, keep + 8, 8, channels)
        land = tiles == LAND
        tiles = jnp.where(land, 0.0, tiles)
        result = mix(tiles, land[:, 4 : 4 + keep], keep, taps, gain[...], up[...], down[...])
        mixed[at, span(tile, tiles_wide)] = result.reshape(at.size, tiles_wide * cols, channels)

    arrived(middle, GROUP - 1)
    mix_chunk(middle * GROUP + 1, GROUP - 2)
    step = 16

    @pl.loop(1, middle)
    def _(q):
        @pl.when(q == middle - 1)
        def _():
            to_ahead.wait_recv()
            to_behind.wait_recv()

            @pl.loop(0, lat_rows // step)
            def _(i):
                rows = pl.ds(i * step, step)
                tiles = jnp.concatenate(
                    [
                        ref[rows].astype(jnp.float32).reshape(step, cols // 8, 8, channels)
                        for ref in (left, masked, right)
                    ],
                    axis=1,
                )
                keep = cols // 8
                land = coded[rows].astype(jnp.float32).reshape(step, keep, 8, channels) == LAND
                result = mix(tiles, land, keep, taps, gain[...], up[...], down[...])
                out_result[rows] = result.reshape(step, cols, channels)

        arrived(middle - q, GROUP)
        arrived(middle + q, GROUP)

        @pl.loop(0, 2)
        def _(side):
            first = side * (middle * GROUP + 7 + (q - 1) * GROUP)
            first += (1 - side) * (middle * GROUP + 1 - q * GROUP)
            mix_chunk(first, GROUP)

    block = CHUNK * cols
    wide = block + 2 * cols
    lane = lax.broadcasted_iota(jnp.int32, (1, 256), 1)
    line = jnp.zeros((1, 256), jnp.float32)
    for k in range(filter_ref.shape[1]):
        line = jnp.where(lane == k + cols - filter_ref.shape[1] // 2, filter_ref[0, k], line)
    weights = pltpu.roll(jnp.broadcast_to(line, (block, 256)), 0, 1, stride=1, stride_axis=0)
    weights = weights[:, :wide]
    high = weights.astype(jnp.bfloat16)
    rest = (weights - high.astype(jnp.float32)).astype(jnp.bfloat16)
    place = mine * GROUP + middle * GROUP + 12

    def block_at(i):
        return pl.ds(pl.multiple_of(lax.rem(place + i * CHUNK, owners) * cols, block), block)

    def filtered(window):
        total = jnp.dot(high, window, preferred_element_type=jnp.float32)
        total += jnp.dot(rest, window, preferred_element_type=jnp.float32)
        return total.astype(jnp.bfloat16)

    blocks = owners // CHUNK
    pieces[:, span(GROUP + owners, 2)] = pieces[:, span(GROUP, 2)]
    mixed[:, span(owners + 9, 4)] = mixed[:, span(9, 4)]

    @pl.loop(0, blocks - 4)
    def _(i):
        window = mixed[:, span(11 + i * CHUNK, CHUNK + 2)]
        result = filtered(jnp.concatenate([window[s] for s in range(SLOTS)], axis=1))
        for s in range(SLOTS):
            polar_result[s, block_at(i)] = result[:, s * channels : (s + 1) * channels]

    arrived(groups, GROUP)
    mix_chunk(owners - 1, GROUP + 2)
    late = range(blocks - 4, blocks)
    windows = [mixed[:, span(11 + i * CHUNK, CHUNK + 2)] for i in late]
    windows = [window[s] for window in windows for s in range(SLOTS)]
    result = filtered(jnp.concatenate(windows, axis=1))
    for k, i in enumerate(late):
        for s in range(SLOTS):
            at = (k * SLOTS + s) * channels
            polar_result[s, block_at(i)] = result[:, at : at + channels]

    to_ahead.wait_send()
    to_behind.wait_send()
    pl.when(hands_left)(pass_left.wait_send)
    pl.when(hands_right)(pass_right.wait_send)
    sent = outgoing.at[pl.ds(0, owners - 1)]
    pltpu.make_async_copy(sent, sent, send_sem.at[0]).wait()


def layer(polar_rows, polar_owner, polar_taps, field, mask, taps, gain, up, down, owners):
    lat_rows, cols, channels = field.shape
    length = owners * cols
    tile = pltpu.VMEM(field.shape, jnp.bfloat16)
    operands = (polar_rows, polar_owner, polar_taps, field, mask, taps, gain, up, down)
    held = [pltpu.VMEM(x.shape, x.dtype) for x in operands]
    held[2] = pltpu.SMEM(polar_taps.shape, polar_taps.dtype)
    return pl.pallas_call(
        layer_kernel,
        out_shape=(
            jax.ShapeDtypeStruct(field.shape, jnp.bfloat16),
            jax.ShapeDtypeStruct((SLOTS, length, channels), jnp.bfloat16),
        ),
        in_specs=[pl.BlockSpec(memory_space=pltpu.HBM)] * len(operands),
        out_specs=(pl.BlockSpec(memory_space=pltpu.VMEM),) * 2,
        scratch_shapes=held
        + [
            pltpu.VMEM((1, SLOTS * owners), jnp.int32),
            pltpu.SMEM((1, SLOTS * owners), jnp.int32),
            pltpu.VMEM((lat_rows + 1, cols, channels), jnp.bfloat16),
            tile,
            tile,
            tile,
            pltpu.VMEM((lat_rows // (GROUP // 2), cols, channels), jnp.bfloat16),
            pltpu.VMEM((owners, SLOTS, cols, channels), jnp.bfloat16),
            pltpu.VMEM((SLOTS, length + 11 * cols, channels), jnp.bfloat16),
            pltpu.VMEM((SLOTS, length + 13 * cols, channels), jnp.bfloat16),
            pltpu.SemaphoreType.DMA((len(operands),)),
            pltpu.SemaphoreType.DMA((1,)),
            pltpu.SemaphoreType.DMA((4,)),
            pltpu.SemaphoreType.DMA((9,)),
            pltpu.SemaphoreType.DMA((3,)),
        ],
        compiler_params=pltpu.CompilerParams(
            collective_id=0, has_side_effects=True, vmem_limit_bytes=32 << 20
        ),
    )(*(pltpu.with_memory_space_constraint(x, pltpu.HBM) for x in operands))


def write_kernel(field_ref, polar_ref, field_out, polar_out, sem):
    parts = sem.shape[0] // 3
    wide, high = polar_ref.shape[1] // (2 * parts), field_ref.shape[0] // parts
    copies = []
    for k in range(2 * parts):
        at = pl.ds(k * wide, wide)
        copies.append(pltpu.make_async_copy(polar_ref.at[:, at], polar_out.at[:, at], sem.at[k]))
    for k in range(parts):
        at = pl.ds(k * high, high)
        copies.append(
            pltpu.make_async_copy(field_ref.at[at], field_out.at[at], sem.at[2 * parts + k])
        )
    for copy in copies:
        copy.start()
    for copy in copies:
        copy.wait()


def write(mixed_field, polar_field):
    return pl.pallas_call(
        write_kernel,
        out_shape=tuple(jax.ShapeDtypeStruct(x.shape, x.dtype) for x in (mixed_field, polar_field)),
        in_specs=[pl.BlockSpec(memory_space=pl.ANY)] * 2,
        out_specs=(pl.BlockSpec(memory_space=pltpu.HBM),) * 2,
        scratch_shapes=[pltpu.SemaphoreType.DMA((6,))],
        compiler_params=pltpu.CompilerParams(vmem_limit_bytes=1 << 20),
    )(mixed_field, polar_field)


def body(field, land_mask, taps, gain, up, down, polar_rows, polar_owner, polar_taps):
    owners = lax.axis_size("lon")
    lists = (polar_rows[None, :], polar_owner[None, :], polar_taps[None, :])
    return write(*layer(*lists, field, land_mask.T, taps, gain[None, :], up, down, owners))


def solution(mesh):
    in_specs = (P("lat", "lon", None), P("lat", "lon"), P(), P(), P(), P(), P("lat"), P("lat"), P())
    out_specs = (P("lat", "lon", None), P(("lat", "lon"), None, None))
    return jax.shard_map(body, mesh=mesh, in_specs=in_specs, out_specs=out_specs, check_vma=False)
```

```python
import jax
import jax.numpy as jnp
from jax import lax
from jax.experimental import pallas as pl
from jax.experimental.pallas import tpu as pltpu
from jax.sharding import PartitionSpec as P

MESH = pl.DeviceIdType.MESH
DILATION = 4
LAND = 64.0
GELU_A = 0.7978845608028654
GELU_B = 0.044715 * GELU_A
GROUP = 8
CHUNK = 4
SLOTS = 2


def mix(tiles, land, keep, taps, gain, half_up, down):
    rows, _, _, channels = tiles.shape
    turned = pltpu.roll(tiles.reshape(rows * (keep + 8), 8, channels), 4, 1).reshape(tiles.shape)
    first_half = lax.broadcasted_iota(jnp.int32, (rows, keep + 7, 8, channels), 2) < 4
    halves = jnp.where(first_half, turned[:, :-1], turned[:, 1:])
    zonal = None
    for k in range(taps.shape[0]):
        start = (k - 7) * DILATION + 32
        source = halves if start % 8 else tiles
        term = taps[k][None, None, None, :] * source[:, start // 8 : start // 8 + keep]
        zonal = term if zonal is None else zonal + term
    zonal = zonal.reshape(rows * keep * 8, channels)
    centred = zonal - jnp.mean(zonal, axis=-1, keepdims=True)
    variance = jnp.mean(centred * centred, axis=-1, keepdims=True)
    normed = (centred * lax.rsqrt(variance + 1e-06) * gain).astype(jnp.bfloat16)
    half = jnp.dot(normed, half_up, preferred_element_type=jnp.float32)
    bend = half * (2 * GELU_A + 8 * GELU_B * (half * half))
    hidden = (half + half * jnp.tanh(bend)).astype(jnp.bfloat16)
    branch = jnp.dot(hidden, down, preferred_element_type=jnp.float32).astype(jnp.bfloat16)
    mixed = tiles[:, 4 : 4 + keep].reshape(-1, channels) + branch.astype(jnp.float32)
    return jnp.where(land.reshape(-1, channels), 0.0, mixed).astype(jnp.bfloat16)


def layer_kernel(
    rows_hbm,
    owner_hbm,
    filter_hbm,
    field_hbm,
    mask_hbm,
    taps_hbm,
    gain_hbm,
    up_hbm,
    down_hbm,
    out_result,
    polar_result,
    listed,
    owner,
    filter_ref,
    field,
    mask,
    taps,
    gain,
    up,
    down,
    table,
    table_ref,
    coded,
    masked,
    left,
    right,
    passing,
    outgoing,
    pieces,
    mixed,
    load_sem,
    store_sem,
    send_sem,
    piece_sem,
    halo_sem,
):
    lat_rows, cols, channels = field.shape
    owners = outgoing.shape[0]
    groups = owners // GROUP
    middle = groups // 2
    band = lax.axis_index("lat")
    me = lax.axis_index("lon")
    mine, low = lax.div(me, GROUP), lax.rem(me, GROUP)
    ahead, behind = lax.rem(me + 1, owners), lax.rem(me + owners - 1, owners)

    loads = [
        pltpu.make_async_copy(source, target, load_sem.at[k])
        for k, (source, target) in enumerate(
            [
                (rows_hbm, listed),
                (owner_hbm, owner),
                (mask_hbm, mask),
                (field_hbm, field),
                (filter_hbm, filter_ref),
                (taps_hbm, taps),
                (gain_hbm, gain),
                (up_hbm, up),
                (down_hbm, down),
            ]
        )
    ]
    barrier = pltpu.get_barrier_semaphore()

    @pl.loop(0, owners // 7)
    def _(i):
        for j in range(7):
            other = lax.rem(me + owners // 2 + 1 + i * 7 + j, owners)
            other = lax.rem(other + jnp.where(other == me, owners // 2, 0), owners)
            pl.semaphore_signal(barrier, inc=1, device_id=(band, other), device_id_type=MESH)

    for load in loads:
        load.start()

    def span(tile, tiles):
        return pl.ds(pl.multiple_of(tile * cols, cols), tiles * cols)

    def piece_copy(position, other):
        relative = lax.rem(position + middle, groups)
        target = lax.rem(mine - relative + groups, groups) * GROUP + lax.rem(low + other, GROUP)
        return pltpu.make_async_remote_copy(
            src_ref=outgoing.at[target],
            dst_ref=pieces.at[:, span(position * GROUP + low, 1)],
            send_sem=send_sem.at[0],
            recv_sem=piece_sem.at[position],
            device_id=(band, target),
            device_id_type=MESH,
        )

    def halo_copy(side, target, k):
        return pltpu.make_async_remote_copy(
            src_ref=masked,
            dst_ref=side,
            send_sem=send_sem.at[1 + k],
            recv_sem=halo_sem.at[k],
            device_id=(band, target),
            device_id_type=MESH,
        )

    loads[0].wait()
    loads[1].wait()
    entries = listed.shape[1]
    shape = (entries, entries)
    entry, earlier = (lax.broadcasted_iota(jnp.int32, shape, k) for k in range(2))
    owners_along = jnp.broadcast_to(owner[...], shape).astype(jnp.float32)
    rows_along = jnp.broadcast_to(listed[...], shape).astype(jnp.float32)

    def total(keep, values):
        return jnp.sum(jnp.where(keep, values, 0.0), axis=1, keepdims=True)

    owner_of = total(entry == earlier, owners_along)
    row_of = total(entry == earlier, rows_along).astype(jnp.int32)
    rank = total((owners_along == owner_of) & (earlier < entry), jnp.ones(shape, jnp.float32))
    place_of = (rank * owners + owner_of).astype(jnp.int32)
    slot = lax.broadcasted_iota(jnp.int32, (entries, SLOTS * owners), 1)
    fill = jnp.where(place_of == slot, row_of - lat_rows, 0)
    table[...] = lat_rows + jnp.sum(fill, axis=0, keepdims=True)
    to_scalars = pltpu.make_async_copy(table, table_ref, store_sem.at[0])
    to_scalars.start()
    loads[2].wait()
    loads[3].wait()
    for r in range(lat_rows):
        wet = jnp.broadcast_to(mask[:, r : r + 1], (cols, channels)) != 0
        values = field[r].astype(jnp.float32)
        coded[r] = jnp.where(wet, values, LAND).astype(jnp.bfloat16)
        masked[r] = jnp.where(wet, values, 0.0).astype(jnp.bfloat16)
    coded[lat_rows] = jnp.full((cols, channels), LAND, jnp.bfloat16)

    to_scalars.wait()

    @pl.loop(0, owners // 4)
    def _(i):
        for j in range(4):
            for s in range(SLOTS):
                outgoing[i * 4 + j, s] = coded[table_ref[0, s * owners + i * 4 + j]]

    pl.semaphore_wait(barrier, owners - 1)
    to_ahead = halo_copy(left, ahead, 0)
    to_behind = halo_copy(right, behind, 1)

    def send(position):
        @pl.loop(1 if position == middle else 0, GROUP)
        def _(other):
            piece_copy(position, other).start()

    parts = GROUP // 2
    quarter = lat_rows // parts
    column = lax.div(low, 2)

    def rows_of(k):
        return pl.ds(k * quarter, quarter)

    def quarter_copy(k, side, step, k_side):
        over = lax.rem(mine + step, groups) * GROUP
        direct = k == (parts - 1 if k_side == 0 else 0)
        target = over + (GROUP - 1 if k_side else 0) if direct else mine * GROUP + 2 * k + 1 - k_side
        return pltpu.make_async_remote_copy(
            src_ref=masked.at[rows_of(k)],
            dst_ref=side.at[rows_of(k)] if direct else passing,
            send_sem=send_sem.at[1 + k_side],
            recv_sem=halo_sem.at[k_side] if direct else halo_sem.at[2],
            device_id=(band, target),
            device_id_type=MESH,
        )

    def hand_on(side, k_side):
        return pltpu.make_async_remote_copy(
            src_ref=passing,
            dst_ref=side.at[rows_of(column)],
            send_sem=send_sem.at[3],
            recv_sem=halo_sem.at[k_side],
            device_id=(
                band,
                lax.rem(mine + (groups - 1 if k_side else 1), groups) * GROUP
                + (GROUP - 1 if k_side else 0),
            ),
            device_id_type=MESH,
        )

    first, final = low == 0, low == GROUP - 1
    inner, outer = low != 0, low != GROUP - 1
    odd = lax.rem(low, 2) == 1
    hands_left = odd & (low < GROUP - 1)
    hands_right = (lax.rem(low, 2) == 0) & (low > 0)
    pass_left, pass_right = hand_on(left, 0), hand_on(right, 1)

    @pl.when(final)
    def _():
        for k in range(parts):
            quarter_copy(k, left, 1, 0).start()

    @pl.when(first)
    def _():
        for k in range(parts):
            quarter_copy(k, right, groups - 1, 1).start()

    send(middle)
    for q in (1, 2):
        send(middle - q)
        send(middle + q)

    @pl.when(hands_left | hands_right)
    def _():
        pltpu.make_async_copy(passing, passing, halo_sem.at[2]).wait()

    pl.when(hands_left)(pass_left.start)
    pl.when(hands_right)(pass_right.start)
    pl.when(outer)(to_ahead.start)
    pl.when(inner)(to_behind.start)
    for q in range(3, middle):
        send(middle - q)
        send(middle + q)
    send(groups)
    pieces[:, span(middle * GROUP + low, 1)] = outgoing[me]
    for load in loads[4:]:
        load.wait()
    half_up = (up[...].astype(jnp.float32) * 0.5).astype(jnp.bfloat16)
    up[...] = half_up

    def arrived(position, tiles):
        landed = pieces.at[:, span(position * GROUP, tiles)]
        pltpu.make_async_copy(landed, landed, piece_sem.at[position]).wait()

    def mix_chunk(tile, tiles_wide, at=pl.ds(0, SLOTS)):
        keep = tiles_wide * cols // 8
        tiles = pieces[at, span(tile - 1, tiles_wide + 2)].astype(jnp.float32)
        tiles = tiles.reshape(at.size, keep + 8, 8, channels)
        land = tiles == LAND
        tiles = jnp.where(land, 0.0, tiles)
        result = mix(tiles, land[:, 4 : 4 + keep], keep, taps, gain[...], up[...], down[...])
        mixed[at, span(tile, tiles_wide)] = result.reshape(at.size, tiles_wide * cols, channels)

    block = CHUNK * cols
    wide = block + 2 * cols
    lane = lax.broadcasted_iota(jnp.int32, (1, 256), 1)
    line = jnp.zeros((1, 256), jnp.float32)
    for k in range(filter_ref.shape[1]):
        line = jnp.where(lane == k + cols - filter_ref.shape[1] // 2, filter_ref[0, k], line)
    weights = pltpu.roll(jnp.broadcast_to(line, (block, 256)), 0, 1, stride=1, stride_axis=0)
    weights = weights[:, :wide]
    high = weights.astype(jnp.bfloat16)
    rest = (weights - high.astype(jnp.float32)).astype(jnp.bfloat16)
    place = mine * GROUP + middle * GROUP + 12

    def block_at(i):
        return pl.ds(pl.multiple_of(lax.rem(place + i * CHUNK, owners) * cols, block), block)

    def filtered(window):
        total = jnp.dot(high, window, preferred_element_type=jnp.float32)
        total += jnp.dot(rest, window, preferred_element_type=jnp.float32)
        return total.astype(jnp.bfloat16)

    def filter_block(i):
        window = mixed[:, span(11 + i * CHUNK, CHUNK + 2)]
        result = filtered(jnp.concatenate([window[s] for s in range(SLOTS)], axis=1))
        for s in range(SLOTS):
            polar_result[s, block_at(i)] = result[:, s * channels : (s + 1) * channels]

    arrived(middle, GROUP - 1)
    mix_chunk(middle * GROUP + 1, GROUP - 2)
    step = 16

    @pl.loop(1, middle)
    def _(q):
        @pl.when(q == middle - 1)
        def _():
            to_ahead.wait_recv()
            to_behind.wait_recv()

            @pl.loop(0, lat_rows // step)
            def _(i):
                rows = pl.ds(i * step, step)
                tiles = jnp.concatenate(
                    [
                        ref[rows].astype(jnp.float32).reshape(step, cols // 8, 8, channels)
                        for ref in (left, masked, right)
                    ],
                    axis=1,
                )
                keep = cols // 8
                land = coded[rows].astype(jnp.float32).reshape(step, keep, 8, channels) == LAND
                result = mix(tiles, land, keep, taps, gain[...], up[...], down[...])
                out_result[rows] = result.reshape(step, cols, channels)

            pl.loop(2, 10)(filter_block)

        arrived(middle - q, GROUP)
        arrived(middle + q, GROUP)

        @pl.loop(0, 2)
        def _(side):
            first = side * (middle * GROUP + 7 + (q - 1) * GROUP)
            first += (1 - side) * (middle * GROUP + 1 - q * GROUP)
            mix_chunk(first, GROUP)

    blocks = owners // CHUNK
    pieces[:, span(GROUP + owners, 2)] = pieces[:, span(GROUP, 2)]
    mixed[:, span(owners + 9, 4)] = mixed[:, span(9, 4)]

    @pl.loop(0, 4)
    def _(k):
        filter_block(k + lax.div(k, 2) * 8)

    arrived(groups, GROUP)
    mix_chunk(owners - 1, GROUP + 2)
    late = range(blocks - 4, blocks)
    windows = [mixed[:, span(11 + i * CHUNK, CHUNK + 2)] for i in late]
    windows = [window[s] for window in windows for s in range(SLOTS)]
    result = filtered(jnp.concatenate(windows, axis=1))
    for k, i in enumerate(late):
        for s in range(SLOTS):
            at = (k * SLOTS + s) * channels
            polar_result[s, block_at(i)] = result[:, at : at + channels]

    to_ahead.wait_send()
    to_behind.wait_send()
    pl.when(hands_left)(pass_left.wait_send)
    pl.when(hands_right)(pass_right.wait_send)
    sent = outgoing.at[pl.ds(0, owners - 1)]
    pltpu.make_async_copy(sent, sent, send_sem.at[0]).wait()


def layer(polar_rows, polar_owner, polar_taps, field, mask, taps, gain, up, down, owners):
    lat_rows, cols, channels = field.shape
    length = owners * cols
    tile = pltpu.VMEM(field.shape, jnp.bfloat16)
    operands = (polar_rows, polar_owner, polar_taps, field, mask, taps, gain, up, down)
    held = [pltpu.VMEM(x.shape, x.dtype) for x in operands]
    held[2] = pltpu.SMEM(polar_taps.shape, polar_taps.dtype)
    return pl.pallas_call(
        layer_kernel,
        out_shape=(
            jax.ShapeDtypeStruct(field.shape, jnp.bfloat16),
            jax.ShapeDtypeStruct((SLOTS, length, channels), jnp.bfloat16),
        ),
        in_specs=[pl.BlockSpec(memory_space=pltpu.HBM)] * len(operands),
        out_specs=(pl.BlockSpec(memory_space=pltpu.VMEM),) * 2,
        scratch_shapes=held
        + [
            pltpu.VMEM((1, SLOTS * owners), jnp.int32),
            pltpu.SMEM((1, SLOTS * owners), jnp.int32),
            pltpu.VMEM((lat_rows + 1, cols, channels), jnp.bfloat16),
            tile,
            tile,
            tile,
            pltpu.VMEM((lat_rows // (GROUP // 2), cols, channels), jnp.bfloat16),
            pltpu.VMEM((owners, SLOTS, cols, channels), jnp.bfloat16),
            pltpu.VMEM((SLOTS, length + 11 * cols, channels), jnp.bfloat16),
            pltpu.VMEM((SLOTS, length + 13 * cols, channels), jnp.bfloat16),
            pltpu.SemaphoreType.DMA((len(operands),)),
            pltpu.SemaphoreType.DMA((1,)),
            pltpu.SemaphoreType.DMA((4,)),
            pltpu.SemaphoreType.DMA((9,)),
            pltpu.SemaphoreType.DMA((3,)),
        ],
        compiler_params=pltpu.CompilerParams(
            collective_id=0, has_side_effects=True, vmem_limit_bytes=32 << 20
        ),
    )(*(pltpu.with_memory_space_constraint(x, pltpu.HBM) for x in operands))


def write_kernel(field_ref, polar_ref, field_out, polar_out, sem):
    parts = sem.shape[0] // 3
    wide, high = polar_ref.shape[1] // (2 * parts), field_ref.shape[0] // parts
    copies = []
    for k in range(2 * parts):
        at = pl.ds(k * wide, wide)
        copies.append(pltpu.make_async_copy(polar_ref.at[:, at], polar_out.at[:, at], sem.at[k]))
    for k in range(parts):
        at = pl.ds(k * high, high)
        copies.append(
            pltpu.make_async_copy(field_ref.at[at], field_out.at[at], sem.at[2 * parts + k])
        )
    for copy in copies:
        copy.start()
    for copy in copies:
        copy.wait()


def write(mixed_field, polar_field):
    return pl.pallas_call(
        write_kernel,
        out_shape=tuple(jax.ShapeDtypeStruct(x.shape, x.dtype) for x in (mixed_field, polar_field)),
        in_specs=[pl.BlockSpec(memory_space=pl.ANY)] * 2,
        out_specs=(pl.BlockSpec(memory_space=pltpu.HBM),) * 2,
        scratch_shapes=[pltpu.SemaphoreType.DMA((6,))],
        compiler_params=pltpu.CompilerParams(vmem_limit_bytes=1 << 20),
    )(mixed_field, polar_field)


def body(field, land_mask, taps, gain, up, down, polar_rows, polar_owner, polar_taps):
    owners = lax.axis_size("lon")
    lists = (polar_rows[None, :], polar_owner[None, :], polar_taps[None, :])
    return write(*layer(*lists, field, land_mask.T, taps, gain[None, :], up, down, owners))


def solution(mesh):
    in_specs = (P("lat", "lon", None), P("lat", "lon"), P(), P(), P(), P(), P("lat"), P("lat"), P())
    out_specs = (P("lat", "lon", None), P(("lat", "lon"), None, None))
    return jax.shard_map(body, mesh=mesh, in_specs=in_specs, out_specs=out_specs, check_vma=False)
```
